256 devices in a mesh: domain: 32 (over x, z), band: 8 (over y, core).
Axes of the slice: x: 4, y: 4, z: 8, core: 2. Of those that a mesh axis runs over, the one named last changes fastest.
Arguments:
- orbitals: float32 [256, 256, 1024], P('band', 'domain'), may hold values from -6 to 6
- seed_index: int32 [256, 1024], P('domain'), may hold values from 0 to 15
- levels: float32 [16], replicated, may hold values from -2 to 2
- group_sizes: int32 [16], replicated, may hold values from 1 to 32, 256 in all
- centres: float32 [16], replicated, may hold values from 4 to 9
Outputs:
- ortho: float32 [256, 256, 1024], P('band', 'domain')
- factor: float32 [256, 256], replicated
The draws below stay inside these ranges and needn't reach their ends.
Inputs may be any that keep to these rules, and one draw needn't show every extreme that they name: `group_sizes`: the 16 group sizes are positive and sum to 256.
All inputs are finite; a program needn't handle non-finite values.
Results may differ from the reference program's by a relative error of at most 0.000096.
Values sent between devices are 32-bit elements; how exact they have to be, the bound alone decides.
A program may use at most 64 MiB of HBM per device.

```python
import math
import jax
import jax.numpy as jnp
import numpy as np
from jax import lax

NY = 32
BANDS = 256
TABLE = 16
GROUPS = 16
GROUP_MOST = 32
NZ = 256
NXY = 1024


def place_ends(result, rng, least, high):
    dims = result.shape
    place = [jax.random.randint(jax.random.fold_in(rng, axis), (), 0, dims[axis]) for axis in range(len(dims))]
    result = result.at[tuple(place)].set(least)
    longest = dims.index(max(dims))
    place[longest] = (place[longest] + 1) % dims[longest]
    return result.at[tuple(place)].set(high)


def block_scale(key, shape, shards, least, largest):
    factor_of = 1.0
    for axis_at, parts in shards:
        draws = jax.random.uniform(jax.random.fold_in(jax.random.fold_in(key, 6), axis_at), (parts,), jnp.float32, least / len(shards), largest / len(shards))
        factor_of = factor_of * jnp.repeat(jnp.exp(draws), shape[axis_at] // parts).reshape((-1,) + (1,) * (len(shape) - 1 - axis_at))
    return factor_of


def length_profile(count, total, reach, slope):
    portions = [(1 << 20) // math.isqrt(rank ** slope) + 1 for rank in range(2, count + 1)]
    surplus, given = total - reach - (count - 1), [1] * (count - 1)
    while surplus > 0:
        free = [i for i in range(count - 1) if given[i] < reach]
        mass, left = sum([portions[i] for i in free]), surplus
        for i in free:
            addition = min(reach - given[i], max(1, left * portions[i] // mass), surplus)
            given[i] = given[i] + addition
            surplus = surplus - addition
    return np.array([reach] + given)


def uneven_parts(own_key, number_of, total, reach, slope):
    if number_of == 2:
        one = jax.random.randint(own_key, (), max(1, total - reach), min(reach, total - 1) + 1)
        return jnp.stack([one, total - one])
    tallies = jnp.asarray(length_profile(number_of, total, reach, slope), jnp.int32)
    pairs = (number_of - 1) // 2
    donor, receiver = tallies[1:1 + 2 * pairs:2], tallies[2:2 + 2 * pairs:2]
    room = jnp.minimum(donor - 1, reach - receiver)
    shifted = jax.random.randint(jax.random.fold_in(own_key, 1), (pairs,), 0, 1 << 20) % (room + 1)
    tallies = tallies.at[1:1 + 2 * pairs:2].set(donor - shifted).at[2:2 + 2 * pairs:2].set(receiver + shifted)
    return tallies[jax.random.permutation(jax.random.fold_in(own_key, 2), number_of)]


def centred(stream_key, shape, deviation, limit, shards=(), kind=jnp.bfloat16):
    level = block_scale(stream_key, shape, shards, -0.22, 0.18) if shards else 1.0
    array = jax.random.normal(stream_key, shape, jnp.float32) * deviation * level
    return jnp.minimum(jnp.maximum(array, -limit), limit).astype(kind)


def setup_inputs(seed: int = 0) -> dict:
    keys = jax.random.split(jax.random.key(seed), 6)
    return {
        "orbitals": centred(keys[0], (BANDS, NZ, NXY), 1.0, 6.0, ((0, 8), (1, 32)), jnp.float32),
        "seed_index": place_ends(jax.random.randint(keys[1], (NZ, NXY), 0, TABLE), jax.random.fold_in(keys[1], 1), 0, TABLE - 1).astype(jnp.int32),
        "levels": jnp.clip(jax.random.uniform(keys[2], (TABLE,), jnp.float32, -2.0, 2.0), -2.0, 2.0),
        "group_sizes": uneven_parts(keys[3], GROUPS, BANDS, GROUP_MOST, 2).astype(jnp.int32),
        "centres": jnp.clip(jax.random.uniform(keys[4], (GROUPS,), jnp.float32, 4.0, 9.0), 4.0, 9.0),
    }


stencil_weights = (-205.0 / 72.0, 8.0 / 5.0, -1.0 / 5.0, 8.0 / 315.0, -1.0 / 560.0)
half_width = 5.0

def shift_cells(field, offset):
    count_all = field.shape[-1]
    pads = [(0, 0)] * (field.ndim - 1)
    if offset > 0:
        return jnp.pad(field[..., offset:], pads + [(0, offset)])
    return jnp.pad(field[..., :count_all + offset], pads + [(-offset, 0)])

def shifted_hamiltonian(extended, potential, centre, row_len):
    planes = extended.shape[1]
    interior = extended[:, 4:planes - 4]
    count_all = interior.shape[-1]
    column = jnp.arange(count_all) % row_len
    summed = 3.0 * stencil_weights[0] * interior
    for distance in range(1, 5):
        weight = stencil_weights[distance]
        along_z = extended[:, 4 + distance:planes - 4 + distance] + extended[:, 4 - distance:planes - 4 - distance]
        along_x = shift_cells(interior, distance * row_len) + shift_cells(interior, -distance * row_len)
        mask_up = (column + distance < row_len).astype(interior.dtype)
        mask_down = (column - distance >= 0).astype(interior.dtype)
        along_y = mask_up * shift_cells(interior, distance) + mask_down * shift_cells(interior, -distance)
        summed = summed + weight * (along_z + along_x + along_y)
    return -0.5 * summed + (potential[None] - centre) * interior

def lookup_potential(seed_index, levels):
    entries = jnp.arange(levels.shape[0]).astype(jnp.int32)
    return jnp.sum(jnp.where(seed_index[None] == entries[:, None, None], levels[:, None, None], 0.0), 0)

def band_centres(group_sizes, centres, band_ids):
    group_ends = jnp.cumsum(group_sizes).astype(jnp.int32)
    member = jnp.sum((group_ends[None, :] <= band_ids[:, None]).astype(jnp.int32), 1)
    groups = jnp.arange(centres.shape[0]).astype(jnp.int32)
    return jnp.sum(jnp.where(member[:, None] == groups[None, :], centres[None, :], 0.0), 1)

def reference(orbitals, seed_index, levels, group_sizes, centres):
    potential = lookup_potential(seed_index, levels)
    centre = band_centres(group_sizes, centres, jnp.arange(BANDS).astype(jnp.int32))
    per_block = BANDS // 16
    pads = ((0, 0), (4, 4), (0, 0))

    def filter_block(pieces):
        band_block, block_centre = pieces
        step_one = shifted_hamiltonian(jnp.pad(band_block, pads), potential, block_centre, NY) / half_width
        return 2.0 * shifted_hamiltonian(jnp.pad(step_one, pads), potential, block_centre, NY) / half_width - band_block
    filtered = lax.map(filter_block, (orbitals.reshape(16, per_block, NZ, NXY), centre.reshape(16, per_block, 1, 1)))
    flattened = filtered.reshape(BANDS, NZ * NXY)
    gram = jnp.dot(flattened.astype(jnp.float32), flattened.T.astype(jnp.float32), precision=lax.Precision.HIGHEST, preferred_element_type=jnp.float32) / (NZ * NXY)
    lower_factor = jnp.linalg.cholesky(gram)
    identity = jnp.eye(BANDS, dtype=gram.dtype)
    inverse = jax.scipy.linalg.solve_triangular(lower_factor, identity, lower=True)
    ortho = jnp.dot(inverse.astype(jnp.float32), flattened.astype(jnp.float32), precision=lax.Precision.HIGHEST, preferred_element_type=jnp.float32)
    return (ortho.reshape(BANDS, NZ, NXY), lower_factor.T)
```

```python
import functools

import jax
import jax.numpy as jnp
from jax import lax
from jax.experimental import pallas as pl
from jax.experimental.pallas import tpu as pltpu
from jax.sharding import PartitionSpec as P

F32 = jnp.float32
MESH = pl.DeviceIdType.MESH
VM = pl.BlockSpec(memory_space=pltpu.VMEM)
SM = pl.BlockSpec(memory_space=pltpu.SMEM)
HIGHEST = lax.Precision.HIGHEST

WEIGHTS = (-205.0 / 72.0, 8.0 / 5.0, -1.0 / 5.0, 8.0 / 315.0, -1.0 / 560.0)
SCALED = tuple(-0.5 / 5.0 * w for w in WEIGHTS)
CHUNKS = 4
XS, ZS = 4, 8


def remote(src, dst, send, recv, domain, band):
    return pltpu.make_async_remote_copy(
        src_ref=src, dst_ref=dst, send_sem=send, recv_sem=recv,
        device_id=(domain, band), device_id_type=MESH,
    )


def nt_dot(a, b):
    return lax.dot_general(
        a, b, (((1,), (1,)), ((), ())), precision=HIGHEST, preferred_element_type=F32
    )


def up(v, r):
    return pltpu.roll(v, 8 - r, 0)


def down(v, r):
    return pltpu.roll(v, r, 0)


def plane_part(v, weights):
    lane = lax.broadcasted_iota(jnp.int32, (8, 128), 1)
    y = lane % 32
    w = weights
    zero = jnp.zeros((8, 128), F32)
    turned = {k: [pltpu.roll(c, 128 - 32 * k, 1) for c in v] for k in (1, 2, 3)}
    out = []
    for c in range(8):
        def beside(k):
            nxt = turned[k][c + 1] if c < 7 else zero
            prv = turned[k][c - 1] if c > 0 else zero
            return jnp.where(lane >= 128 - 32 * k, nxt, prv)

        s = w[2] * (turned[2][c] + beside(2))
        s += jnp.where(lane < 96, w[1], w[3]) * turned[1][c]
        s += jnp.where(lane >= 96, w[1], w[3]) * beside(1)
        s += jnp.where(lane < 32, w[3], w[1]) * turned[3][c]
        s += jnp.where(lane >= 32, w[3], w[1]) * beside(3)
        far = (v[c + 1] if c < 7 else zero) + (v[c - 1] if c > 0 else zero)
        s += w[4] * far
        for r in range(1, 5):
            s += jnp.where(y + r < 32, w[r], 0.0) * pltpu.roll(v[c], 128 - r, 1)
            s += jnp.where(y - r >= 0, w[r], 0.0) * pltpu.roll(v[c], r, 1)
        out.append(s)
    return out


def filter_band(own, prv, nxt, pot_own, pot_edge, centre, edge_mask):
    w = SCALED
    row = lax.broadcasted_iota(jnp.int32, (8, 128), 0)
    edge = [jnp.where(row < 4, n, p) for n, p in zip(nxt, prv)]
    flat_own = plane_part(own, w)
    flat_edge = plane_part(edge, w)
    one_own, one_edge = [], []
    for c in range(8):
        o, p, n, e = own[c], prv[c], nxt[c], edge[c]
        s = flat_own[c]
        t = flat_edge[c]
        for r in range(1, 4):
            above = up(jnp.where(row >= r, o, n), r)
            below = down(jnp.where(row < 8 - r, o, p), r)
            s += w[r] * (above + below)
            above = up(jnp.where(row < r, o, jnp.where(row < r + 4, n, p)), r)
            below = down(jnp.where(row >= 8 - r, o, jnp.where(row < 4 - r, n, p)), r)
            t += w[r] * (above + below)
        s += w[4] * down(jnp.where(row >= 4, o, n) + jnp.where(row < 4, o, p), 4)
        t += w[4] * down(jnp.where(row < 4, o, n) + jnp.where(row >= 4, o, p), 4)
        s += (3.0 * w[0] + 0.2 * (pot_own[c] - centre)) * o
        t += (3.0 * w[0] + 0.2 * (pot_edge[c] - centre)) * e
        one_own.append(s)
        one_edge.append(t * edge_mask)
    flat = plane_part(one_own, w)
    out = []
    for c in range(8):
        o, e = one_own[c], one_edge[c]
        s = flat[c]
        for r in range(1, 4):
            above = up(jnp.where(row >= r, o, e), r)
            below = down(jnp.where(row < 8 - r, o, e), r)
            s += w[r] * (above + below)
        s += w[4] * down(o + e, 4)
        s += (3.0 * w[0] + 0.2 * (pot_own[c] - centre)) * o
        out.append(2.0 * s - own[c])
    return out


def columns(ref, lead=()):
    return [ref[(*lead, slice(None), slice(128 * c, 128 * c + 128))] for c in range(8)]


def gather_kernel(
    orb, seed, levels, sizes, centres,
    field, gram,
    prv, nxt, seed_edge, pot, pot_edge, filt, local, band_in, zsum_in, xsum_in, share,
    centre_of,
    halo_send, halo_recv, seed_send, seed_recv, swap_send, swap_recv,
    rs_send, rs_recv, z_send, z_recv, x_send, x_recv, zg_send, zg_recv, g_send, g_recv,
):
    dom, me = lax.axis_index("domain"), lax.axis_index("band")
    x, z = dom // ZS, dom % ZS
    has_prev, has_next = dom > 0, dom < XS * ZS - 1
    per = 32 // CHUNKS

    barrier = pltpu.get_barrier_semaphore()

    def greet(d, b):
        pl.semaphore_signal(barrier, inc=1, device_id=(d, b), device_id_type=MESH)

    outer_prev = jnp.logical_and(has_prev, z == 0)
    outer_next = jnp.logical_and(has_next, z == ZS - 1)
    pl.when(outer_prev)(lambda: greet(dom - 1, me))
    pl.when(outer_next)(lambda: greet(dom + 1, me))
    for j in range(1, 8):
        greet(x * ZS + (z + j) % ZS, me)
        greet(dom, (me + j) % 8)
    for j in range(1, XS):
        greet(((x + j) % XS) * ZS + z, me)

    total = sizes[0]
    ends = [total]
    for g in range(1, 15):
        total = total + sizes[g]
        ends.append(total)

    def one_centre(b, carry):
        value = centres[0]
        for g in range(15):
            value = jnp.where(ends[g] <= me * 32 + b, centres[g + 1], value)
        centre_of[b] = value
        return carry

    lax.fori_loop(0, 32, one_centre, 0)

    def lookup(index):
        value = jnp.zeros(index.shape, F32)
        for t in range(16):
            value = jnp.where(index == t, levels[t], value)
        return value

    pot[...] = lookup(seed[...])

    @pl.when(jnp.logical_not(has_prev))
    def _():
        prv[...] = jnp.zeros_like(prv)
        seed_edge[4:8, :] = jnp.zeros((4, 1024), jnp.int32)

    @pl.when(jnp.logical_not(has_next))
    def _():
        nxt[...] = jnp.zeros_like(nxt)
        seed_edge[0:4, :] = jnp.zeros((4, 1024), jnp.int32)

    one = jnp.int32(1)
    pl.semaphore_wait(barrier, 17 + jnp.where(outer_prev, one, 0) + jnp.where(outer_next, one, 0))

    def to_next(ch):
        part = pl.ds(per * ch, per)
        return remote(orb.at[part], prv.at[part], halo_send.at[0, ch], halo_recv.at[0, ch], dom + 1, me)

    def to_prev(ch):
        part = pl.ds(per * ch, per)
        return remote(orb.at[part], nxt.at[part], halo_send.at[1, ch], halo_recv.at[1, ch], dom - 1, me)

    def seed_next():
        return remote(seed.at[pl.ds(4, 4)], seed_edge.at[pl.ds(4, 4)], seed_send.at[0], seed_recv.at[0], dom + 1, me)

    def seed_prev():
        return remote(seed.at[pl.ds(0, 4)], seed_edge.at[pl.ds(0, 4)], seed_send.at[1], seed_recv.at[1], dom - 1, me)

    @pl.when(has_next)
    def _():
        seed_next().start()
        for ch in range(CHUNKS):
            to_next(ch).start()

    @pl.when(has_prev)
    def _():
        seed_prev().start()
        for ch in range(CHUNKS):
            to_prev(ch).start()

    pl.when(has_prev)(lambda: seed_next().wait_recv())
    pl.when(has_next)(lambda: seed_prev().wait_recv())
    pot_edge[...] = lookup(seed_edge[...])

    row = lax.broadcasted_iota(jnp.int32, (8, 128), 0)
    keep_next = jnp.where(has_next, 1.0, 0.0)
    keep_prev = jnp.where(has_prev, 1.0, 0.0)
    edge_mask = jnp.where(row < 4, keep_next, keep_prev)

    def swap(j, ch):
        peer = (me + j) % 8
        lanes = pl.ds(pl.multiple_of(peer * 128, 128), 128)
        return remote(
            filt.at[pl.ds(per * ch, per), :, lanes],
            field.at[pl.ds(32 * me + per * ch, per)],
            swap_send.at[j - 1, ch], swap_recv.at[j - 1, ch], dom, peer,
        )

    for ch in range(CHUNKS):
        pl.when(has_prev)(lambda: to_next(ch).wait_recv())
        pl.when(has_next)(lambda: to_prev(ch).wait_recv())

        def one_band(b, carry):
            out = filter_band(
                columns(orb, (b,)), columns(prv, (b,)), columns(nxt, (b,)),
                columns(pot), columns(pot_edge), centre_of[b], edge_mask,
            )
            for c in range(8):
                filt[b, :, 128 * c : 128 * c + 128] = out[c]
            return carry

        lax.fori_loop(per * ch, per * ch + per, one_band, 0)
        for j in range(1, 8):
            swap(j, ch).start()

    mine = pl.ds(pl.multiple_of(me * 128, 128), 128)
    field[pl.ds(32 * me, 32)] = filt[:, :, mine]
    for ch in range(CHUNKS):
        for j in range(1, 8):
            swap(j, ch).wait_recv()

    total_gram = None
    for k in range(8):
        part = field[:, k, :]
        term = nt_dot(part, part)
        total_gram = term if total_gram is None else total_gram + term
    local[...] = total_gram

    def rs(j):
        peer = (me + j) % 8
        return remote(
            local.at[pl.ds(pl.multiple_of(32 * peer, 32), 32)], band_in.at[me],
            rs_send.at[j - 1], rs_recv.at[j - 1], dom, peer,
        )

    for j in range(1, 8):
        rs(j).start()
    band_in[me] = local[pl.ds(pl.multiple_of(32 * me, 32), 32), :]
    for j in range(1, 8):
        rs(j).wait_recv()
    acc = band_in[0]
    for k in range(1, 8):
        acc = acc + band_in[k]
    for k in range(8):
        share[k] = acc[4 * k : 4 * k + 4]

    def zsum(j):
        peer = (z + j) % ZS
        return remote(share.at[peer], zsum_in.at[z], z_send.at[j - 1], z_recv.at[j - 1], x * ZS + peer, me)

    for j in range(1, ZS):
        zsum(j).start()
    zsum_in[z] = share[z]
    for j in range(1, ZS):
        zsum(j).wait_recv()
    acc = zsum_in[0]
    for k in range(1, ZS):
        acc = acc + zsum_in[k]
    xsum_in[x] = acc

    def xsum(j):
        peer = (x + j) % XS
        return remote(xsum_in.at[x], xsum_in.at[x], x_send.at[j - 1], x_recv.at[j - 1], peer * ZS + z, me)

    for j in range(1, XS):
        xsum(j).start()
    for j in range(1, XS):
        xsum(j).wait_recv()
    acc = xsum_in[0]
    for k in range(1, XS):
        acc = acc + xsum_in[k]
    gram[8 * me + z] = acc

    def zgather(j):
        peer = (z + j) % ZS
        here = gram.at[8 * me + z]
        return remote(here, here, zg_send.at[j - 1], zg_recv.at[j - 1], x * ZS + peer, me)

    for j in range(1, ZS):
        zgather(j).start()
    for j in range(1, ZS):
        zgather(j).wait_recv()

    def bgather(j):
        peer = (me + j) % 8
        here = gram.at[pl.ds(8 * me, 8)]
        return remote(here, here, g_send.at[j - 1], g_recv.at[j - 1], dom, peer)

    for j in range(1, 8):
        bgather(j).start()
    for j in range(1, 8):
        bgather(j).wait_recv()

    pl.when(has_next)(lambda: seed_next().wait_send())
    pl.when(has_prev)(lambda: seed_prev().wait_send())
    for ch in range(CHUNKS):
        pl.when(has_next)(lambda: to_next(ch).wait_send())
        pl.when(has_prev)(lambda: to_prev(ch).wait_send())
        for j in range(1, 8):
            swap(j, ch).wait_send()
    for j in range(1, 8):
        rs(j).wait_send()
        bgather(j).wait_send()
    for j in range(1, ZS):
        zsum(j).wait_send()
        zgather(j).wait_send()
    for j in range(1, XS):
        xsum(j).wait_send()


def gather_call(orb, seed, levels, sizes, centres):
    dma = pltpu.SemaphoreType.DMA
    block = pltpu.VMEM((32, 8, 1024), F32)
    return pl.pallas_call(
        gather_kernel,
        out_shape=(
            jax.ShapeDtypeStruct((256, 8, 128), F32),
            jax.ShapeDtypeStruct((64, 4, 256), F32),
        ),
        in_specs=[VM, VM, SM, SM, SM],
        out_specs=(VM, VM),
        scratch_shapes=[
            block, block, pltpu.VMEM((8, 1024), jnp.int32),
            pltpu.VMEM((8, 1024), F32), pltpu.VMEM((8, 1024), F32), block,
            pltpu.VMEM((256, 256), F32), pltpu.VMEM((8, 32, 256), F32),
            pltpu.VMEM((ZS, 4, 256), F32), pltpu.VMEM((XS, 4, 256), F32), pltpu.VMEM((8, 4, 256), F32),
            pltpu.SMEM((32,), F32),
            dma((2, CHUNKS)), dma((2, CHUNKS)), dma((2,)), dma((2,)),
            dma((7, CHUNKS)), dma((7, CHUNKS)),
            dma((7,)), dma((7,)), dma((7,)), dma((7,)), dma((3,)), dma((3,)),
            dma((7,)), dma((7,)), dma((7,)), dma((7,)),
        ],
        compiler_params=pltpu.CompilerParams(
            collective_id=0, has_side_effects=True, vmem_limit_bytes=48 << 20
        ),
        name="filter_and_gram",
    )(orb, seed, levels, sizes, centres)


def return_kernel(inverse, field, out, rows, send, recv):
    dom, me = lax.axis_index("domain"), lax.axis_index("band")
    barrier = pltpu.get_barrier_semaphore()
    for j in range(1, 8):
        pl.semaphore_signal(barrier, inc=1, device_id=(dom, (me + j) % 8), device_id_type=MESH)
    for k in range(8):
        rows[:, k, :] = jnp.dot(
            inverse[...], field[:, k, :], precision=HIGHEST, preferred_element_type=F32
        )
    pl.semaphore_wait(barrier, 7)
    mine = pl.ds(pl.multiple_of(me * 128, 128), 128)

    def give(j):
        peer = (me + j) % 8
        return remote(
            rows.at[pl.ds(32 * peer, 32)], out.at[:, :, mine],
            send.at[j - 1], recv.at[j - 1], dom, peer,
        )

    for j in range(1, 8):
        give(j).start()
    out[:, :, mine] = rows[pl.ds(32 * me, 32)]
    for j in range(1, 8):
        give(j).wait()


def return_call(inverse, field):
    dma = pltpu.SemaphoreType.DMA
    return pl.pallas_call(
        return_kernel,
        out_shape=jax.ShapeDtypeStruct((32, 8, 1024), F32),
        in_specs=[VM, VM],
        out_specs=VM,
        scratch_shapes=[pltpu.VMEM((256, 8, 128), F32), dma((7,)), dma((7,))],
        compiler_params=pltpu.CompilerParams(
            collective_id=1, has_side_effects=True, vmem_limit_bytes=32 << 20
        ),
        name="ortho_and_return",
    )(inverse, field)


def shards(orbitals, seed_index, levels, group_sizes, centres):
    field, gram_sum = gather_call(orbitals, seed_index, levels, group_sizes, centres)
    gram = gram_sum.reshape(256, 256) / (256 * 1024)
    lower = jnp.linalg.cholesky(gram)
    identity = jnp.eye(256, dtype=F32)
    inverse = jax.scipy.linalg.solve_triangular(lower, identity, lower=True)
    return return_call(inverse, field), lower.T


def solution(mesh):
    in_specs = (P("band", "domain", None), P("domain", None), P(), P(), P())
    out_specs = (P("band", "domain", None), P())
    return jax.shard_map(
        shards, mesh=mesh, in_specs=in_specs, out_specs=out_specs, check_vma=False
    )
```

```python
import functools

import jax
import jax.numpy as jnp
from jax import lax
from jax.experimental import pallas as pl
from jax.experimental.pallas import tpu as pltpu
from jax.sharding import PartitionSpec as P

F32 = jnp.float32
MESH = pl.DeviceIdType.MESH
VM = pl.BlockSpec(memory_space=pltpu.VMEM)
SM = pl.BlockSpec(memory_space=pltpu.SMEM)
HIGHEST = lax.Precision.HIGHEST

WEIGHTS = (-205.0 / 72.0, 8.0 / 5.0, -1.0 / 5.0, 8.0 / 315.0, -1.0 / 560.0)
SCALED = tuple(-0.5 / 5.0 * w for w in WEIGHTS)
CHUNKS = 4
BLOCK = 64
XS, ZS = 4, 8


def remote(src, dst, send, recv, domain, band):
    return pltpu.make_async_remote_copy(
        src_ref=src, dst_ref=dst, send_sem=send, recv_sem=recv,
        device_id=(domain, band), device_id_type=MESH,
    )


def nt_dot(a, b):
    return lax.dot_general(
        a, b, (((1,), (1,)), ((), ())), precision=HIGHEST, preferred_element_type=F32
    )


def nn_dot(a, b):
    return jnp.dot(a, b, precision=HIGHEST, preferred_element_type=F32)


def up(v, r):
    return pltpu.roll(v, 8 - r, 0)


def down(v, r):
    return pltpu.roll(v, r, 0)


def plane_part(v, weights):
    lane = lax.broadcasted_iota(jnp.int32, (8, 128), 1)
    y = lane % 32
    w = weights
    zero = jnp.zeros((8, 128), F32)
    turned = {k: [pltpu.roll(c, 128 - 32 * k, 1) for c in v] for k in (1, 2, 3)}
    out = []
    for c in range(8):
        def beside(k):
            nxt = turned[k][c + 1] if c < 7 else zero
            prv = turned[k][c - 1] if c > 0 else zero
            return jnp.where(lane >= 128 - 32 * k, nxt, prv)

        s = w[2] * (turned[2][c] + beside(2))
        s += jnp.where(lane < 96, w[1], w[3]) * turned[1][c]
        s += jnp.where(lane >= 96, w[1], w[3]) * beside(1)
        s += jnp.where(lane < 32, w[3], w[1]) * turned[3][c]
        s += jnp.where(lane >= 32, w[3], w[1]) * beside(3)
        far = (v[c + 1] if c < 7 else zero) + (v[c - 1] if c > 0 else zero)
        s += w[4] * far
        for r in range(1, 5):
            s += jnp.where(y + r < 32, w[r], 0.0) * pltpu.roll(v[c], 128 - r, 1)
            s += jnp.where(y - r >= 0, w[r], 0.0) * pltpu.roll(v[c], r, 1)
        out.append(s)
    return out


def filter_band(own, prv, nxt, pot_own, pot_edge, centre, edge_mask):
    w = SCALED
    row = lax.broadcasted_iota(jnp.int32, (8, 128), 0)
    edge = [jnp.where(row < 4, n, p) for n, p in zip(nxt, prv)]
    flat_own = plane_part(own, w)
    flat_edge = plane_part(edge, w)
    one_own, one_edge = [], []
    for c in range(8):
        o, p, n, e = own[c], prv[c], nxt[c], edge[c]
        s = flat_own[c]
        t = flat_edge[c]
        for r in range(1, 4):
            above = up(jnp.where(row >= r, o, n), r)
            below = down(jnp.where(row < 8 - r, o, p), r)
            s += w[r] * (above + below)
            above = up(jnp.where(row < r, o, jnp.where(row < r + 4, n, p)), r)
            below = down(jnp.where(row >= 8 - r, o, jnp.where(row < 4 - r, n, p)), r)
            t += w[r] * (above + below)
        s += w[4] * down(jnp.where(row >= 4, o, n) + jnp.where(row < 4, o, p), 4)
        t += w[4] * down(jnp.where(row < 4, o, n) + jnp.where(row >= 4, o, p), 4)
        s += (3.0 * w[0] + 0.2 * (pot_own[c] - centre)) * o
        t += (3.0 * w[0] + 0.2 * (pot_edge[c] - centre)) * e
        one_own.append(s)
        one_edge.append(t * edge_mask)
    flat = plane_part(one_own, w)
    out = []
    for c in range(8):
        o, e = one_own[c], one_edge[c]
        s = flat[c]
        for r in range(1, 4):
            above = up(jnp.where(row >= r, o, e), r)
            below = down(jnp.where(row < 8 - r, o, e), r)
            s += w[r] * (above + below)
        s += w[4] * down(o + e, 4)
        s += (3.0 * w[0] + 0.2 * (pot_own[c] - centre)) * o
        out.append(2.0 * s - own[c])
    return out


def columns(ref, lead=()):
    return [ref[(*lead, slice(None), slice(128 * c, 128 * c + 128))] for c in range(8)]


def gather_kernel(
    orb, seed, levels, sizes, centres,
    field, gram,
    prv, nxt, seed_edge, pot, pot_edge, filt, local, band_in, zsum_in, xsum_in, share,
    centre_of,
    halo_send, halo_recv, seed_send, seed_recv, swap_send, swap_recv,
    rs_send, rs_recv, z_send, z_recv, x_send, x_recv, zg_send, zg_recv, g_send, g_recv,
):
    dom, me = lax.axis_index("domain"), lax.axis_index("band")
    x, z = dom // ZS, dom % ZS
    has_prev, has_next = dom > 0, dom < XS * ZS - 1
    per = 32 // CHUNKS

    barrier = pltpu.get_barrier_semaphore()

    def greet(d, b):
        pl.semaphore_signal(barrier, inc=1, device_id=(d, b), device_id_type=MESH)

    outer_prev = jnp.logical_and(has_prev, z == 0)
    outer_next = jnp.logical_and(has_next, z == ZS - 1)
    pl.when(outer_prev)(lambda: greet(dom - 1, me))
    pl.when(outer_next)(lambda: greet(dom + 1, me))
    for j in range(1, 8):
        greet(x * ZS + (z + j) % ZS, me)
        greet(dom, (me + j) % 8)
    for j in range(1, XS):
        greet(((x + j) % XS) * ZS + z, me)

    total = sizes[0]
    ends = [total]
    for g in range(1, 15):
        total = total + sizes[g]
        ends.append(total)

    def one_centre(b, carry):
        value = centres[0]
        for g in range(15):
            value = jnp.where(ends[g] <= me * 32 + b, centres[g + 1], value)
        centre_of[b] = value
        return carry

    lax.fori_loop(0, 32, one_centre, 0)

    def lookup(index):
        value = jnp.zeros(index.shape, F32)
        for t in range(16):
            value = jnp.where(index == t, levels[t], value)
        return value

    pot[...] = lookup(seed[...])

    @pl.when(jnp.logical_not(has_prev))
    def _():
        prv[...] = jnp.zeros_like(prv)
        seed_edge[4:8, :] = jnp.zeros((4, 1024), jnp.int32)

    @pl.when(jnp.logical_not(has_next))
    def _():
        nxt[...] = jnp.zeros_like(nxt)
        seed_edge[0:4, :] = jnp.zeros((4, 1024), jnp.int32)

    one = jnp.int32(1)
    pl.semaphore_wait(barrier, 17 + jnp.where(outer_prev, one, 0) + jnp.where(outer_next, one, 0))

    def to_next(ch):
        part = pl.ds(per * ch, per)
        return remote(orb.at[part], prv.at[part], halo_send.at[0, ch], halo_recv.at[0, ch], dom + 1, me)

    def to_prev(ch):
        part = pl.ds(per * ch, per)
        return remote(orb.at[part], nxt.at[part], halo_send.at[1, ch], halo_recv.at[1, ch], dom - 1, me)

    def seed_next():
        return remote(seed.at[pl.ds(4, 4)], seed_edge.at[pl.ds(4, 4)], seed_send.at[0], seed_recv.at[0], dom + 1, me)

    def seed_prev():
        return remote(seed.at[pl.ds(0, 4)], seed_edge.at[pl.ds(0, 4)], seed_send.at[1], seed_recv.at[1], dom - 1, me)

    @pl.when(has_next)
    def _():
        seed_next().start()
        for ch in range(CHUNKS):
            to_next(ch).start()

    @pl.when(has_prev)
    def _():
        seed_prev().start()
        for ch in range(CHUNKS):
            to_prev(ch).start()

    pl.when(has_prev)(lambda: seed_next().wait_recv())
    pl.when(has_next)(lambda: seed_prev().wait_recv())
    pot_edge[...] = lookup(seed_edge[...])

    row = lax.broadcasted_iota(jnp.int32, (8, 128), 0)
    keep_next = jnp.where(has_next, 1.0, 0.0)
    keep_prev = jnp.where(has_prev, 1.0, 0.0)
    edge_mask = jnp.where(row < 4, keep_next, keep_prev)

    def swap(j, ch):
        peer = (me + j) % 8
        lanes = pl.ds(pl.multiple_of(peer * 128, 128), 128)
        return remote(
            filt.at[pl.ds(per * ch, per), :, lanes],
            field.at[pl.ds(32 * me + per * ch, per)],
            swap_send.at[j - 1, ch], swap_recv.at[j - 1, ch], dom, peer,
        )

    for ch in range(CHUNKS):
        pl.when(has_prev)(lambda: to_next(ch).wait_recv())
        pl.when(has_next)(lambda: to_prev(ch).wait_recv())

        def one_band(b, carry):
            out = filter_band(
                columns(orb, (b,)), columns(prv, (b,)), columns(nxt, (b,)),
                columns(pot), columns(pot_edge), centre_of[b], edge_mask,
            )
            for c in range(8):
                filt[b, :, 128 * c : 128 * c + 128] = out[c]
            return carry

        lax.fori_loop(per * ch, per * ch + per, one_band, 0)
        for j in range(1, 8):
            swap(j, ch).start()

    mine = pl.ds(pl.multiple_of(me * 128, 128), 128)
    field[pl.ds(32 * me, 32)] = filt[:, :, mine]
    for ch in range(CHUNKS):
        for j in range(1, 8):
            swap(j, ch).wait_recv()

    total_gram = None
    for k in range(8):
        part = field[:, k, :]
        term = nt_dot(part, part)
        total_gram = term if total_gram is None else total_gram + term
    local[...] = total_gram

    def rs(j):
        peer = (me + j) % 8
        return remote(
            local.at[pl.ds(pl.multiple_of(32 * peer, 32), 32)], band_in.at[me],
            rs_send.at[j - 1], rs_recv.at[j - 1], dom, peer,
        )

    for j in range(1, 8):
        rs(j).start()
    band_in[me] = local[pl.ds(pl.multiple_of(32 * me, 32), 32), :]
    for j in range(1, 8):
        rs(j).wait_recv()
    acc = band_in[0]
    for k in range(1, 8):
        acc = acc + band_in[k]
    for k in range(8):
        share[k] = acc[8 * (k // 2) : 8 * (k // 2) + 8, 128 * (k % 2) : 128 * (k % 2) + 128]

    def zsum(j):
        peer = (z + j) % ZS
        return remote(share.at[peer], zsum_in.at[z], z_send.at[j - 1], z_recv.at[j - 1], x * ZS + peer, me)

    for j in range(1, ZS):
        zsum(j).start()
    zsum_in[z] = share[z]
    for j in range(1, ZS):
        zsum(j).wait_recv()
    acc = zsum_in[0]
    for k in range(1, ZS):
        acc = acc + zsum_in[k]
    xsum_in[x] = acc

    def xsum(j):
        peer = (x + j) % XS
        return remote(xsum_in.at[x], xsum_in.at[x], x_send.at[j - 1], x_recv.at[j - 1], peer * ZS + z, me)

    for j in range(1, XS):
        xsum(j).start()
    for j in range(1, XS):
        xsum(j).wait_recv()
    acc = xsum_in[0]
    for k in range(1, XS):
        acc = acc + xsum_in[k]
    piece = gram.at[
        pl.ds(pl.multiple_of(32 * me + 8 * (z // 2), 8), 8), pl.ds(pl.multiple_of(128 * (z % 2), 128), 128)
    ]
    piece[...] = acc

    def zgather(j):
        peer = (z + j) % ZS
        return remote(piece, piece, zg_send.at[j - 1], zg_recv.at[j - 1], x * ZS + peer, me)

    for j in range(1, ZS):
        zgather(j).start()
    for j in range(1, ZS):
        zgather(j).wait_recv()

    def bgather(j):
        peer = (me + j) % 8
        here = gram.at[pl.ds(pl.multiple_of(32 * me, 32), 32)]
        return remote(here, here, g_send.at[j - 1], g_recv.at[j - 1], dom, peer)

    for j in range(1, 8):
        bgather(j).start()
    for j in range(1, 8):
        bgather(j).wait_recv()

    pl.when(has_next)(lambda: seed_next().wait_send())
    pl.when(has_prev)(lambda: seed_prev().wait_send())
    for ch in range(CHUNKS):
        pl.when(has_next)(lambda: to_next(ch).wait_send())
        pl.when(has_prev)(lambda: to_prev(ch).wait_send())
        for j in range(1, 8):
            swap(j, ch).wait_send()
    for j in range(1, 8):
        rs(j).wait_send()
        bgather(j).wait_send()
    for j in range(1, ZS):
        zsum(j).wait_send()
        zgather(j).wait_send()
    for j in range(1, XS):
        xsum(j).wait_send()


def gather_call(orb, seed, levels, sizes, centres):
    dma = pltpu.SemaphoreType.DMA
    block = pltpu.VMEM((32, 8, 1024), F32)
    return pl.pallas_call(
        gather_kernel,
        out_shape=(
            jax.ShapeDtypeStruct((256, 8, 128), F32),
            jax.ShapeDtypeStruct((256, 256), F32),
        ),
        in_specs=[VM, VM, SM, SM, SM],
        out_specs=(VM, VM),
        scratch_shapes=[
            block, block, pltpu.VMEM((8, 1024), jnp.int32),
            pltpu.VMEM((8, 1024), F32), pltpu.VMEM((8, 1024), F32), block,
            pltpu.VMEM((256, 256), F32), pltpu.VMEM((8, 32, 256), F32),
            pltpu.VMEM((ZS, 8, 128), F32), pltpu.VMEM((XS, 8, 128), F32), pltpu.VMEM((8, 8, 128), F32),
            pltpu.SMEM((32,), F32),
            dma((2, CHUNKS)), dma((2, CHUNKS)), dma((2,)), dma((2,)),
            dma((7, CHUNKS)), dma((7, CHUNKS)),
            dma((7,)), dma((7,)), dma((7,)), dma((7,)), dma((3,)), dma((3,)),
            dma((7,)), dma((7,)), dma((7,)), dma((7,)),
        ],
        compiler_params=pltpu.CompilerParams(
            collective_id=0, has_side_effects=True, vmem_limit_bytes=48 << 20
        ),
        name="filter_and_gram",
    )(orb, seed, levels, sizes, centres)


def eliminate(diag):
    row = lax.broadcasted_iota(jnp.int32, (8, 128), 0)
    lane = lax.broadcasted_iota(jnp.int32, (8, 128), 1)
    groups = BLOCK // 8
    a = []
    for i in range(groups):
        unit = jnp.where(lane == row + (BLOCK + 8 * i), 1.0, 0.0)
        a.append(jnp.where(lane < BLOCK, diag[i], unit))
    for p in range(groups):
        spread = [
            [jnp.broadcast_to(a[i][:, 8 * p + l : 8 * p + l + 1], (8, 128)) for i in range(p, groups)]
            for l in range(8)
        ]
        for k in range(8):
            first = spread[k][0]
            inv = 1.0 / first[k : k + 1, :]
            mult = [jnp.where(row > k, first, 0.0)] + spread[k][1:]
            for l in range(k + 1, 8):
                s = spread[l][0][k : k + 1, :] * inv
                spread[l] = [v - m * s for v, m in zip(spread[l], mult)]
            pivot_row = a[p][k : k + 1, :] * inv
            for i in range(p, groups):
                a[i] = a[i] - mult[i - p] * pivot_row
    out = []
    for i in range(groups):
        d = jnp.sum(jnp.where(lane == row + 8 * i, a[i], 0.0), axis=1, keepdims=True)
        scaled = a[i] * lax.rsqrt(d)
        out.append(jnp.where(jnp.logical_or(lane >= BLOCK, lane >= row + 8 * i), scaled, 0.0))
    return out

def factor_kernel(gram, factor, inverse, m, duo):
    n = 256
    scale = 1.0 / (256 * 1024)
    m[...] = gram[...] * scale
    factor[...] = jnp.zeros((n, n), F32)
    inverse[...] = jnp.zeros((n, n), F32)
    for j in range(n // BLOCK):
        lo, hi = j * BLOCK, (j + 1) * BLOCK
        base = lo // 128 * 128
        diag = []
        for i in range(BLOCK // 8):
            d = m[lo + 8 * i : lo + 8 * i + 8, base : base + 128]
            if lo != base:
                d = pltpu.roll(d, 128 - (lo - base), 1)
            diag.append(d)
        done = eliminate(diag)
        for i in range(BLOCK // 8):
            duo[8 * i : 8 * i + 8, :] = done[i]
        r_jj, w_jj = duo[:, :BLOCK], duo[:, BLOCK:]
        new = nn_dot(w_jj, m[lo:hi, :])
        if lo:
            inverse[lo:hi, :lo] = new[:, :lo]
        inverse[lo:hi, lo:hi] = w_jj
        factor[lo:hi, lo:hi] = r_jj
        if hi < n:
            factor[lo:hi, hi:] = new[:, hi:]
            left = nt_dot(m[hi:, lo:hi], w_jj)
            m[lo:hi, :] = new
            m[lo:hi, lo:hi] = w_jj
            m[hi:, lo:hi] = jnp.zeros((n - hi, BLOCK), F32)
            m[hi:, :] = m[hi:, :] - nn_dot(left, m[lo:hi, :])

def factor_call(gram):
    sq = jax.ShapeDtypeStruct((256,256),F32)
    return pl.pallas_call(factor_kernel, out_shape=(sq,sq), in_specs=[VM], out_specs=(VM,VM),
        scratch_shapes=[pltpu.VMEM((256,256),F32), pltpu.VMEM((64,128),F32)], name="factor_and_inverse")(gram)


def return_kernel(inverse, field, out, rows, send, recv):
    dom, me = lax.axis_index("domain"), lax.axis_index("band")
    barrier = pltpu.get_barrier_semaphore()
    for j in range(1, 8):
        pl.semaphore_signal(barrier, inc=1, device_id=(dom, (me + j) % 8), device_id_type=MESH)
    for k in range(8):
        rows[:, k, :] = jnp.dot(
            inverse[...], field[:, k, :], precision=HIGHEST, preferred_element_type=F32
        )
    pl.semaphore_wait(barrier, 7)
    mine = pl.ds(pl.multiple_of(me * 128, 128), 128)

    def give(j):
        peer = (me + j) % 8
        return remote(
            rows.at[pl.ds(32 * peer, 32)], out.at[:, :, mine],
            send.at[j - 1], recv.at[j - 1], dom, peer,
        )

    for j in range(1, 8):
        give(j).start()
    out[:, :, mine] = rows[pl.ds(32 * me, 32)]
    for j in range(1, 8):
        give(j).wait()


def return_call(inverse, field):
    dma = pltpu.SemaphoreType.DMA
    return pl.pallas_call(
        return_kernel,
        out_shape=jax.ShapeDtypeStruct((32, 8, 1024), F32),
        in_specs=[VM, VM],
        out_specs=VM,
        scratch_shapes=[pltpu.VMEM((256, 8, 128), F32), dma((7,)), dma((7,))],
        compiler_params=pltpu.CompilerParams(
            collective_id=1, has_side_effects=True, vmem_limit_bytes=32 << 20
        ),
        name="ortho_and_return",
    )(inverse, field)


def shards(orbitals, seed_index, levels, group_sizes, centres):
    field, gram_sum = gather_call(orbitals, seed_index, levels, group_sizes, centres)
    factor, inverse = factor_call(gram_sum)
    return return_call(inverse, field), factor


def solution(mesh):
    in_specs = (P("band", "domain", None), P("domain", None), P(), P(), P())
    out_specs = (P("band", "domain", None), P())
    return jax.shard_map(
        shards, mesh=mesh, in_specs=in_specs, out_specs=out_specs, check_vma=False
    )
```

```python
import functools

import jax
import jax.numpy as jnp
from jax import lax
from jax.experimental import pallas as pl
from jax.experimental.pallas import tpu as pltpu
from jax.sharding import PartitionSpec as P

F32 = jnp.float32
MESH = pl.DeviceIdType.MESH
VM = pl.BlockSpec(memory_space=pltpu.VMEM)
SM = pl.BlockSpec(memory_space=pltpu.SMEM)
HIGHEST = lax.Precision.HIGHEST

WEIGHTS = (-205.0 / 72.0, 8.0 / 5.0, -1.0 / 5.0, 8.0 / 315.0, -1.0 / 560.0)
SCALED = tuple(-0.5 / 5.0 * w for w in WEIGHTS)
CUTS = (0, 8, 16, 24, 28, 30, 32)
CHUNKS = len(CUTS) - 1
BLOCK = 64
XS, ZS = 4, 8


def remote(src, dst, send, recv, domain, band):
    return pltpu.make_async_remote_copy(
        src_ref=src, dst_ref=dst, send_sem=send, recv_sem=recv,
        device_id=(domain, band), device_id_type=MESH,
    )


def nt_dot(a, b):
    return lax.dot_general(
        a, b, (((1,), (1,)), ((), ())), precision=HIGHEST, preferred_element_type=F32
    )


def nn_dot(a, b):
    return jnp.dot(a, b, precision=HIGHEST, preferred_element_type=F32)


def up(v, r):
    return pltpu.roll(v, 8 - r, 0)


def down(v, r):
    return pltpu.roll(v, r, 0)


def plane_part(v, weights):
    lane = lax.broadcasted_iota(jnp.int32, (8, 128), 1)
    y = lane % 32
    w = weights
    zero = jnp.zeros((8, 128), F32)
    turned = {k: [pltpu.roll(c, 128 - 32 * k, 1) for c in v] for k in (1, 2, 3)}
    out = []
    for c in range(8):
        def beside(k):
            nxt = turned[k][c + 1] if c < 7 else zero
            prv = turned[k][c - 1] if c > 0 else zero
            return jnp.where(lane >= 128 - 32 * k, nxt, prv)

        s = w[2] * (turned[2][c] + beside(2))
        s += jnp.where(lane < 96, w[1], w[3]) * turned[1][c]
        s += jnp.where(lane >= 96, w[1], w[3]) * beside(1)
        s += jnp.where(lane < 32, w[3], w[1]) * turned[3][c]
        s += jnp.where(lane >= 32, w[3], w[1]) * beside(3)
        far = (v[c + 1] if c < 7 else zero) + (v[c - 1] if c > 0 else zero)
        s += w[4] * far
        for r in range(1, 5):
            s += jnp.where(y + r < 32, w[r], 0.0) * pltpu.roll(v[c], 128 - r, 1)
            s += jnp.where(y - r >= 0, w[r], 0.0) * pltpu.roll(v[c], r, 1)
        out.append(s)
    return out


def filter_band(own, prv, nxt, pot_own, pot_edge, centre, edge_mask):
    w = SCALED
    row = lax.broadcasted_iota(jnp.int32, (8, 128), 0)
    edge = [jnp.where(row < 4, n, p) for n, p in zip(nxt, prv)]
    flat_own = plane_part(own, w)
    flat_edge = plane_part(edge, w)
    one_own, one_edge = [], []
    for c in range(8):
        o, p, n, e = own[c], prv[c], nxt[c], edge[c]
        s = flat_own[c]
        t = flat_edge[c]
        for r in range(1, 4):
            above = up(jnp.where(row >= r, o, n), r)
            below = down(jnp.where(row < 8 - r, o, p), r)
            s += w[r] * (above + below)
            above = up(jnp.where(row < r, o, jnp.where(row < r + 4, n, p)), r)
            below = down(jnp.where(row >= 8 - r, o, jnp.where(row < 4 - r, n, p)), r)
            t += w[r] * (above + below)
        s += w[4] * down(jnp.where(row >= 4, o, n) + jnp.where(row < 4, o, p), 4)
        t += w[4] * down(jnp.where(row < 4, o, n) + jnp.where(row >= 4, o, p), 4)
        s += (3.0 * w[0] + 0.2 * (pot_own[c] - centre)) * o
        t += (3.0 * w[0] + 0.2 * (pot_edge[c] - centre)) * e
        one_own.append(s)
        one_edge.append(t * edge_mask)
    flat = plane_part(one_own, w)
    out = []
    for c in range(8):
        o, e = one_own[c], one_edge[c]
        s = flat[c]
        for r in range(1, 4):
            above = up(jnp.where(row >= r, o, e), r)
            below = down(jnp.where(row < 8 - r, o, e), r)
            s += w[r] * (above + below)
        s += w[4] * down(o + e, 4)
        s += (3.0 * w[0] + 0.2 * (pot_own[c] - centre)) * o
        out.append(2.0 * s - own[c])
    return out


def columns(ref, lead=()):
    return [ref[(*lead, slice(None), slice(128 * c, 128 * c + 128))] for c in range(8)]


def eliminate(diag):
    row = lax.broadcasted_iota(jnp.int32, (8, 128), 0)
    lane = lax.broadcasted_iota(jnp.int32, (8, 128), 1)
    groups = BLOCK // 8
    a = []
    for i in range(groups):
        unit = jnp.where(lane == row + (BLOCK + 8 * i), 1.0, 0.0)
        a.append(jnp.where(lane < BLOCK, diag[i], unit))
    for p in range(groups):
        spread = [
            [jnp.broadcast_to(a[i][:, 8 * p + l : 8 * p + l + 1], (8, 128)) for i in range(p, groups)]
            for l in range(8)
        ]
        for k in range(8):
            first = spread[k][0]
            inv = 1.0 / first[k : k + 1, :]
            mult = [jnp.where(row > k, first, 0.0)] + spread[k][1:]
            for l in range(k + 1, 8):
                s = spread[l][0][k : k + 1, :] * inv
                spread[l] = [v - m * s for v, m in zip(spread[l], mult)]
            pivot_row = a[p][k : k + 1, :] * inv
            for i in range(p, groups):
                a[i] = a[i] - mult[i - p] * pivot_row
    out = []
    for i in range(groups):
        d = jnp.sum(jnp.where(lane == row + 8 * i, a[i], 0.0), axis=1, keepdims=True)
        scaled = a[i] * lax.rsqrt(d)
        out.append(jnp.where(jnp.logical_or(lane >= BLOCK, lane >= row + 8 * i), scaled, 0.0))
    return out

def step_kernel(
    orb_h, seed_h, levels_h, sizes_h, centres_h,
    out, factor,
    levels, sizes, centres, orb, seed, prv, nxt, seed_edge, pot, pot_edge, centre_of, filt,
    field, dense, local, band_in, share, zsum_in, xsum_in, m, lower, duo, done, rows,
    in_sem, hello, halo_send, halo_recv, seed_send, seed_recv, swap_send, swap_recv,
    rs_send, rs_recv, z_send, z_recv, x_send, x_recv, zg_send, zg_recv, g_send, g_recv,
    give_send, give_recv,
):
    dom, me = lax.axis_index("domain"), lax.axis_index("band")
    x, z = dom // ZS, dom % ZS
    has_prev, has_next = dom > 0, dom < XS * ZS - 1

    barrier = pltpu.get_barrier_semaphore()

    def greet(d, b):
        pl.semaphore_signal(barrier, inc=1, device_id=(d, b), device_id_type=MESH)

    outer_prev = jnp.logical_and(has_prev, z == 0)
    outer_next = jnp.logical_and(has_next, z == ZS - 1)
    pl.when(outer_prev)(lambda: greet(dom - 1, me))
    pl.when(outer_next)(lambda: greet(dom + 1, me))
    for j in (1, 7, 2, 6):
        greet(x * ZS + (z + j) % ZS, me)
    for j in range(1, 8):
        greet(dom, (me + j) % 8)
    for j in range(1, XS):
        greet(((x + j) % XS) * ZS + z, me)

    loads = [
        pltpu.make_async_copy(levels_h, levels, in_sem.at[0]),
        pltpu.make_async_copy(sizes_h, sizes, in_sem.at[1]),
        pltpu.make_async_copy(centres_h, centres, in_sem.at[2]),
        pltpu.make_async_copy(seed_h, seed, in_sem.at[3]),
        pltpu.make_async_copy(orb_h, orb, in_sem.at[4]),
    ]
    for load in loads:
        load.start()

    @pl.when(jnp.logical_not(has_prev))
    def _():
        prv[...] = jnp.zeros_like(prv)
        seed_edge[4:8, :] = jnp.zeros((4, 1024), jnp.int32)

    @pl.when(jnp.logical_not(has_next))
    def _():
        nxt[...] = jnp.zeros_like(nxt)
        seed_edge[0:4, :] = jnp.zeros((4, 1024), jnp.int32)

    one = jnp.int32(1)
    pl.semaphore_wait(barrier, 14 + jnp.where(outer_prev, one, 0) + jnp.where(outer_next, one, 0))

    def to_next(ch):
        part = pl.ds(CUTS[ch], CUTS[ch + 1] - CUTS[ch])
        return remote(orb_h.at[part], prv.at[part], halo_send.at[0, ch], halo_recv.at[0, ch], dom + 1, me)

    def to_prev(ch):
        part = pl.ds(CUTS[ch], CUTS[ch + 1] - CUTS[ch])
        return remote(orb_h.at[part], nxt.at[part], halo_send.at[1, ch], halo_recv.at[1, ch], dom - 1, me)

    def seed_next():
        return remote(seed.at[pl.ds(4, 4)], seed_edge.at[pl.ds(4, 4)], seed_send.at[0], seed_recv.at[0], dom + 1, me)

    def seed_prev():
        return remote(seed.at[pl.ds(0, 4)], seed_edge.at[pl.ds(0, 4)], seed_send.at[1], seed_recv.at[1], dom - 1, me)

    loads[3].wait()

    @pl.when(has_next)
    def _():
        seed_next().start()
        for ch in range(CHUNKS):
            to_next(ch).start()

    @pl.when(has_prev)
    def _():
        seed_prev().start()
        for ch in range(CHUNKS):
            to_prev(ch).start()

    for j in (2, 6):
        pl.semaphore_signal(hello, inc=1, device_id=(x * ZS + (z + j) % ZS, me), device_id_type=MESH)

    for load in loads[:3] + loads[4:]:
        load.wait()

    def lookup(index):
        value = jnp.zeros(index.shape, F32)
        for t in range(16):
            value = jnp.where(index == t, levels[t], value)
        return value

    pot[...] = lookup(seed[...])
    band = lax.broadcasted_iota(jnp.int32, (32, 128), 0) + 32 * me
    total = sizes[0]
    value = jnp.full((32, 128), centres[0], F32)
    for g in range(15):
        value = jnp.where(total <= band, centres[g + 1], value)
        total = total + sizes[g + 1]
    centre_of[...] = value

    pl.when(has_prev)(lambda: seed_next().wait_recv())
    pl.when(has_next)(lambda: seed_prev().wait_recv())
    pot_edge[...] = lookup(seed_edge[...])

    row = lax.broadcasted_iota(jnp.int32, (8, 128), 0)
    keep_next = jnp.where(has_next, 1.0, 0.0)
    keep_prev = jnp.where(has_prev, 1.0, 0.0)
    edge_mask = jnp.where(row < 4, keep_next, keep_prev)

    def swap(j, ch):
        peer = (me + j) % 8
        lanes = pl.ds(pl.multiple_of(peer * 128, 128), 128)
        count = CUTS[ch + 1] - CUTS[ch]
        return remote(
            filt.at[pl.ds(CUTS[ch], count), :, lanes],
            field.at[pl.ds(32 * me + CUTS[ch], count)],
            swap_send.at[j - 1, ch], swap_recv.at[j - 1, ch], dom, peer,
        )

    for ch in range(CHUNKS):
        pl.when(has_prev)(lambda: to_next(ch).wait_recv())
        pl.when(has_next)(lambda: to_prev(ch).wait_recv())

        def one_band(b, carry):
            new = filter_band(
                columns(orb, (b,)), columns(prv, (b,)), columns(nxt, (b,)),
                columns(pot), columns(pot_edge), centre_of[pl.ds(b, 1), :], edge_mask,
            )
            for c in range(8):
                filt[b, :, 128 * c : 128 * c + 128] = new[c]
            return carry

        lax.fori_loop(CUTS[ch], CUTS[ch + 1], one_band, 0)
        for j in range(1, 8):
            swap(j, ch).start()

    mine = pl.ds(pl.multiple_of(me * 128, 128), 128)
    field[pl.ds(32 * me, 32)] = filt[:, :, mine]
    pl.semaphore_wait(hello, 2)
    for ch in range(CHUNKS):
        for j in range(1, 8):
            swap(j, ch).wait_recv()

    total_gram = None
    for k in range(0, 8, 2):
        part = jnp.concatenate([field[:, k, :], field[:, k + 1, :]], axis=1)
        dense[:, 128 * k : 128 * k + 256] = part
        term = nt_dot(part, part)
        total_gram = term if total_gram is None else total_gram + term
    local[...] = total_gram

    def rs(j):
        peer = (me + j) % 8
        return remote(
            local.at[pl.ds(pl.multiple_of(32 * peer, 32), 32)], band_in.at[me],
            rs_send.at[j - 1], rs_recv.at[j - 1], dom, peer,
        )

    for j in range(1, 8):
        rs(j).start()
    band_in[me] = local[pl.ds(pl.multiple_of(32 * me, 32), 32), :]
    for j in range(1, 8):
        rs(j).wait_recv()
    acc = band_in[0]
    for k in range(1, 8):
        acc = acc + band_in[k]
    for k in range(8):
        share[k] = acc[8 * (k // 2) : 8 * (k // 2) + 8, 128 * (k % 2) : 128 * (k % 2) + 128]

    def zsum(j):
        peer = (z + j) % ZS
        return remote(share.at[peer], zsum_in.at[z], z_send.at[j - 1], z_recv.at[j - 1], x * ZS + peer, me)

    for j in range(1, ZS):
        zsum(j).start()
    zsum_in[z] = share[z]
    for j in range(1, ZS):
        zsum(j).wait_recv()
    acc = zsum_in[0]
    for k in range(1, ZS):
        acc = acc + zsum_in[k]
    xsum_in[x] = acc

    def xsum(j):
        peer = (x + j) % XS
        return remote(xsum_in.at[x], xsum_in.at[x], x_send.at[j - 1], x_recv.at[j - 1], peer * ZS + z, me)

    for j in range(1, XS):
        xsum(j).start()
    for j in range(1, XS):
        xsum(j).wait_recv()
    acc = xsum_in[0]
    for k in range(1, XS):
        acc = acc + xsum_in[k]
    piece = m.at[
        pl.ds(pl.multiple_of(32 * me + 8 * (z // 2), 8), 8), pl.ds(pl.multiple_of(128 * (z % 2), 128), 128)
    ]
    piece[...] = acc * (1.0 / (256 * 1024))

    def zgather(j):
        peer = (z + j) % ZS
        return remote(piece, piece, zg_send.at[j - 1], zg_recv.at[j - 1], x * ZS + peer, me)

    for j in range(1, ZS):
        zgather(j).start()
    for j in range(1, ZS):
        zgather(j).wait_recv()

    def bgather(j):
        peer = (me + j) % 8
        here = m.at[pl.ds(pl.multiple_of(32 * me, 32), 32)]
        return remote(here, here, g_send.at[j - 1], g_recv.at[j - 1], dom, peer)

    for j in range(1, 8):
        bgather(j).start()
    factor[...] = jnp.zeros((256, 256), F32)
    for j in range(1, 8):
        bgather(j).wait_recv()
    for j in range(1, ZS):
        zgather(j).wait_send()
    for j in range(1, 8):
        bgather(j).wait_send()

    def give(d):
        j = (d - me + 8) % 8
        return remote(
            rows.at[pl.ds(32 * d, 32)], out.at[:, :, mine], give_send.at[j], give_recv.at[j], dom, d
        )

    n = 256
    for blk in range(n // BLOCK):
        lo, hi = blk * BLOCK, (blk + 1) * BLOCK
        base = lo // 128 * 128
        diag = []
        for i in range(BLOCK // 8):
            d = m[lo + 8 * i : lo + 8 * i + 8, base : base + 128]
            if lo != base:
                d = pltpu.roll(d, 128 - (lo - base), 1)
            diag.append(d)
        rest = dense[lo:hi, :]
        if lo:
            rest = rest - nn_dot(lower[lo:hi, :lo], done[:lo, :])
        both = eliminate(diag)
        for i in range(BLOCK // 8):
            duo[8 * i : 8 * i + 8, :] = both[i]
        r_jj, w_jj = duo[:, :BLOCK], duo[:, BLOCK:]
        factor[lo:hi, lo:hi] = r_jj
        if hi < n:
            new = nn_dot(w_jj, m[lo:hi, :])[:, hi:]
            factor[lo:hi, hi:] = new
            left = nt_dot(m[hi:, lo:hi], w_jj)
            lower[hi:, lo:hi] = left
            m[hi:, hi:] = m[hi:, hi:] - nn_dot(left, new)
        solved = nn_dot(w_jj, rest)
        done[lo:hi, :] = solved
        for k in range(8):
            rows[lo:hi, k, :] = solved[:, 128 * k : 128 * k + 128]
        for d in (2 * blk, 2 * blk + 1):
            pl.when(me != d)(lambda: give(d).start())

    out[:, :, mine] = rows[pl.ds(32 * me, 32)]

    pl.when(has_next)(lambda: seed_next().wait_send())
    pl.when(has_prev)(lambda: seed_prev().wait_send())
    for ch in range(CHUNKS):
        pl.when(has_next)(lambda: to_next(ch).wait_send())
        pl.when(has_prev)(lambda: to_prev(ch).wait_send())
        for j in range(1, 8):
            swap(j, ch).wait_send()
    for j in range(1, 8):
        rs(j).wait_send()
    for j in range(1, ZS):
        zsum(j).wait_send()
    for j in range(1, XS):
        xsum(j).wait_send()
    for d in range(8):
        pl.when(me != d)(lambda: give(d).wait_send())
    for j in range(1, 8):
        remote(
            rows.at[pl.ds(0, 32)], out.at[:, :, mine], give_send.at[j], give_recv.at[j], dom, (me + j) % 8
        ).wait_recv()


def step_call(orb, seed, levels, sizes, centres):
    dma = pltpu.SemaphoreType.DMA
    vmem = pltpu.VMEM
    block = vmem((32, 8, 1024), F32)
    plane = vmem((8, 1024), F32)
    square = vmem((256, 256), F32)
    hbm = pl.BlockSpec(memory_space=pltpu.MemorySpace.HBM)
    return pl.pallas_call(
        step_kernel,
        out_shape=(
            jax.ShapeDtypeStruct((32, 8, 1024), F32),
            jax.ShapeDtypeStruct((256, 256), F32),
        ),
        in_specs=[hbm] * 5,
        out_specs=(VM, VM),
        scratch_shapes=[
            pltpu.SMEM((16,), F32), pltpu.SMEM((16,), jnp.int32), pltpu.SMEM((16,), F32),
            block, vmem((8, 1024), jnp.int32), block, block, vmem((8, 1024), jnp.int32),
            plane, plane, vmem((32, 128), F32), block,
            vmem((256, 8, 128), F32), vmem((256, 1024), F32), square, vmem((8, 32, 256), F32),
            vmem((8, 8, 128), F32), vmem((ZS, 8, 128), F32), vmem((XS, 8, 128), F32),
            square, square, vmem((BLOCK, 128), F32), vmem((256, 1024), F32), vmem((256, 8, 128), F32),
            dma((5,)), pltpu.SemaphoreType.REGULAR,
            dma((2, CHUNKS)), dma((2, CHUNKS)), dma((2,)), dma((2,)),
            dma((7, CHUNKS)), dma((7, CHUNKS)),
            dma((7,)), dma((7,)), dma((7,)), dma((7,)), dma((3,)), dma((3,)),
            dma((7,)), dma((7,)), dma((7,)), dma((7,)), dma((8,)), dma((8,)),
        ],
        compiler_params=pltpu.CompilerParams(
            collective_id=0, has_side_effects=True, vmem_limit_bytes=24 << 20
        ),
        name="filtered_step",
    )(*(pltpu.with_memory_space_constraint(a, pltpu.HBM) for a in (orb, seed, levels, sizes, centres)))


def shards(orbitals, seed_index, levels, group_sizes, centres):
    return step_call(orbitals, seed_index, levels, group_sizes, centres)


def solution(mesh):
    in_specs = (P("band", "domain", None), P("domain", None), P(), P(), P())
    out_specs = (P("band", "domain", None), P())
    return jax.shard_map(
        shards, mesh=mesh, in_specs=in_specs, out_specs=out_specs, check_vma=False
    )
```

```python
import functools

import jax
import jax.numpy as jnp
from jax import lax
from jax.experimental import pallas as pl
from jax.experimental.pallas import tpu as pltpu
from jax.sharding import PartitionSpec as P

F32 = jnp.float32
MESH = pl.DeviceIdType.MESH
VM = pl.BlockSpec(memory_space=pltpu.VMEM)
SM = pl.BlockSpec(memory_space=pltpu.SMEM)
HIGHEST = lax.Precision.HIGHEST

WEIGHTS = (-205.0 / 72.0, 8.0 / 5.0, -1.0 / 5.0, 8.0 / 315.0, -1.0 / 560.0)
SCALED = tuple(-0.5 / 5.0 * w for w in WEIGHTS)
CUTS = (0, 8, 16, 24, 28, 30, 32)
CHUNKS = len(CUTS) - 1
BLOCK = 64
PANEL = 16
XS, ZS = 4, 8


def remote(src, dst, send, recv, domain, band):
    return pltpu.make_async_remote_copy(
        src_ref=src, dst_ref=dst, send_sem=send, recv_sem=recv,
        device_id=(domain, band), device_id_type=MESH,
    )


def nt_dot(a, b):
    return lax.dot_general(
        a, b, (((1,), (1,)), ((), ())), precision=HIGHEST, preferred_element_type=F32
    )


def nn_dot(a, b):
    return jnp.dot(a, b, precision=HIGHEST, preferred_element_type=F32)


def up(v, r):
    return pltpu.roll(v, 8 - r, 0)


def down(v, r):
    return pltpu.roll(v, r, 0)


def plane_part(v, weights):
    lane = lax.broadcasted_iota(jnp.int32, (8, 128), 1)
    y = lane % 32
    w = weights
    zero = jnp.zeros((8, 128), F32)
    turned = {k: [pltpu.roll(c, 128 - 32 * k, 1) for c in v] for k in (1, 2, 3)}
    out = []
    for c in range(8):
        def beside(k):
            nxt = turned[k][c + 1] if c < 7 else zero
            prv = turned[k][c - 1] if c > 0 else zero
            return jnp.where(lane >= 128 - 32 * k, nxt, prv)

        s = w[2] * (turned[2][c] + beside(2))
        s += jnp.where(lane < 96, w[1], w[3]) * turned[1][c]
        s += jnp.where(lane >= 96, w[1], w[3]) * beside(1)
        s += jnp.where(lane < 32, w[3], w[1]) * turned[3][c]
        s += jnp.where(lane >= 32, w[3], w[1]) * beside(3)
        far = (v[c + 1] if c < 7 else zero) + (v[c - 1] if c > 0 else zero)
        s += w[4] * far
        for r in range(1, 5):
            s += jnp.where(y + r < 32, w[r], 0.0) * pltpu.roll(v[c], 128 - r, 1)
            s += jnp.where(y - r >= 0, w[r], 0.0) * pltpu.roll(v[c], r, 1)
        out.append(s)
    return out


def filter_band(own, prv, nxt, pot_own, pot_edge, centre, edge_mask):
    w = SCALED
    row = lax.broadcasted_iota(jnp.int32, (8, 128), 0)
    edge = [jnp.where(row < 4, n, p) for n, p in zip(nxt, prv)]
    flat_own = plane_part(own, w)
    flat_edge = plane_part(edge, w)
    one_own, one_edge = [], []
    for c in range(8):
        o, p, n, e = own[c], prv[c], nxt[c], edge[c]
        s = flat_own[c]
        t = flat_edge[c]
        for r in range(1, 4):
            above = up(jnp.where(row >= r, o, n), r)
            below = down(jnp.where(row < 8 - r, o, p), r)
            s += w[r] * (above + below)
            above = up(jnp.where(row < r, o, jnp.where(row < r + 4, n, p)), r)
            below = down(jnp.where(row >= 8 - r, o, jnp.where(row < 4 - r, n, p)), r)
            t += w[r] * (above + below)
        s += w[4] * down(jnp.where(row >= 4, o, n) + jnp.where(row < 4, o, p), 4)
        t += w[4] * down(jnp.where(row < 4, o, n) + jnp.where(row >= 4, o, p), 4)
        s += (3.0 * w[0] + 0.2 * (pot_own[c] - centre)) * o
        t += (3.0 * w[0] + 0.2 * (pot_edge[c] - centre)) * e
        one_own.append(s)
        one_edge.append(t * edge_mask)
    flat = plane_part(one_own, w)
    out = []
    for c in range(8):
        o, e = one_own[c], one_edge[c]
        s = flat[c]
        for r in range(1, 4):
            above = up(jnp.where(row >= r, o, e), r)
            below = down(jnp.where(row < 8 - r, o, e), r)
            s += w[r] * (above + below)
        s += w[4] * down(o + e, 4)
        s += (3.0 * w[0] + 0.2 * (pot_own[c] - centre)) * o
        out.append(2.0 * s - own[c])
    return out


def columns(ref, lead=()):
    return [ref[(*lead, slice(None), slice(128 * c, 128 * c + 128))] for c in range(8)]


def eliminate(diag):
    row = lax.broadcasted_iota(jnp.int32, (8, 128), 0)
    lane = lax.broadcasted_iota(jnp.int32, (8, 128), 1)
    groups = BLOCK // 8
    a = []
    for i in range(groups):
        unit = jnp.where(lane == row + (BLOCK + 8 * i), 1.0, 0.0)
        a.append(jnp.where(lane < BLOCK, diag[i], unit))
    step = PANEL // 8
    for p in range(0, groups, step):
        spread = [
            [jnp.broadcast_to(a[i][:, 8 * p + l : 8 * p + l + 1], (8, 128)) for i in range(p, groups)]
            for l in range(PANEL)
        ]
        for k in range(PANEL):
            g, at = k // 8, k % 8
            first = spread[k][g]
            inv = 1.0 / first[at : at + 1, :]
            mult = [jnp.where(row > at, first, 0.0)] + spread[k][g + 1 :]
            for l in range(k + 1, PANEL):
                t = spread[l][g][at : at + 1, :] * inv
                spread[l] = spread[l][:g] + [v - m * t for v, m in zip(spread[l][g:], mult)]
            pivot_row = a[p + g][at : at + 1, :] * inv
            for i in range(p + g, groups):
                a[i] = a[i] - mult[i - p - g] * pivot_row
    out = []
    for i in range(groups):
        d = jnp.sum(jnp.where(lane == row + 8 * i, a[i], 0.0), axis=1, keepdims=True)
        scaled = a[i] * lax.rsqrt(d)
        out.append(jnp.where(jnp.logical_or(lane >= BLOCK, lane >= row + 8 * i), scaled, 0.0))
    return out

def step_kernel(
    orb_h, seed_h, levels_h, sizes_h, centres_h,
    out, factor,
    levels, sizes, centres, orb, seed, prv, nxt, seed_edge, pot, pot_edge, centre_of, filt,
    field, dense, local, band_in, share, zsum_in, parts_in, m, lower, duo, done, rows,
    in_sem, hello, halo_send, halo_recv, seed_send, seed_recv, swap_send, swap_recv,
    rs_send, rs_recv, z_send, z_recv, part_send, part_recv, g_send, g_recv,
    give_send, give_recv,
):
    dom, me = lax.axis_index("domain"), lax.axis_index("band")
    x, z = dom // ZS, dom % ZS
    has_prev, has_next = dom > 0, dom < XS * ZS - 1

    barrier = pltpu.get_barrier_semaphore()

    def greet(d, b):
        pl.semaphore_signal(barrier, inc=1, device_id=(d, b), device_id_type=MESH)

    outer_prev = jnp.logical_and(has_prev, z == 0)
    outer_next = jnp.logical_and(has_next, z == ZS - 1)
    pl.when(outer_prev)(lambda: greet(dom - 1, me))
    pl.when(outer_next)(lambda: greet(dom + 1, me))
    for j in (1, 7, 2, 6):
        greet(x * ZS + (z + j) % ZS, me)
    for j in range(1, 8):
        greet(dom, (me + j) % 8)
    for j in range(1, XS):
        greet(((x + j) % XS) * ZS + z, me)

    loads = [
        pltpu.make_async_copy(levels_h, levels, in_sem.at[0]),
        pltpu.make_async_copy(sizes_h, sizes, in_sem.at[1]),
        pltpu.make_async_copy(centres_h, centres, in_sem.at[2]),
        pltpu.make_async_copy(seed_h, seed, in_sem.at[3]),
        pltpu.make_async_copy(orb_h, orb, in_sem.at[4]),
    ]
    for load in loads:
        load.start()

    @pl.when(jnp.logical_not(has_prev))
    def _():
        prv[...] = jnp.zeros_like(prv)
        seed_edge[4:8, :] = jnp.zeros((4, 1024), jnp.int32)

    @pl.when(jnp.logical_not(has_next))
    def _():
        nxt[...] = jnp.zeros_like(nxt)
        seed_edge[0:4, :] = jnp.zeros((4, 1024), jnp.int32)

    one = jnp.int32(1)
    pl.semaphore_wait(barrier, 14 + jnp.where(outer_prev, one, 0) + jnp.where(outer_next, one, 0))

    def to_next(ch):
        part = pl.ds(CUTS[ch], CUTS[ch + 1] - CUTS[ch])
        return remote(orb_h.at[part], prv.at[part], halo_send.at[0, ch], halo_recv.at[0, ch], dom + 1, me)

    def to_prev(ch):
        part = pl.ds(CUTS[ch], CUTS[ch + 1] - CUTS[ch])
        return remote(orb_h.at[part], nxt.at[part], halo_send.at[1, ch], halo_recv.at[1, ch], dom - 1, me)

    def seed_next():
        return remote(seed.at[pl.ds(4, 4)], seed_edge.at[pl.ds(4, 4)], seed_send.at[0], seed_recv.at[0], dom + 1, me)

    def seed_prev():
        return remote(seed.at[pl.ds(0, 4)], seed_edge.at[pl.ds(0, 4)], seed_send.at[1], seed_recv.at[1], dom - 1, me)

    loads[3].wait()

    @pl.when(has_next)
    def _():
        seed_next().start()
        for ch in range(CHUNKS):
            to_next(ch).start()

    @pl.when(has_prev)
    def _():
        seed_prev().start()
        for ch in range(CHUNKS):
            to_prev(ch).start()

    for j in (2, 6):
        pl.semaphore_signal(hello, inc=1, device_id=(x * ZS + (z + j) % ZS, me), device_id_type=MESH)

    for load in loads[:3] + loads[4:]:
        load.wait()

    def lookup(index):
        value = jnp.zeros(index.shape, F32)
        for t in range(16):
            value = jnp.where(index == t, levels[t], value)
        return value

    pot[...] = lookup(seed[...])
    band = lax.broadcasted_iota(jnp.int32, (32, 128), 0) + 32 * me
    total = sizes[0]
    value = jnp.full((32, 128), centres[0], F32)
    for g in range(15):
        value = jnp.where(total <= band, centres[g + 1], value)
        total = total + sizes[g + 1]
    centre_of[...] = value

    pl.when(has_prev)(lambda: seed_next().wait_recv())
    pl.when(has_next)(lambda: seed_prev().wait_recv())
    pot_edge[...] = lookup(seed_edge[...])

    row = lax.broadcasted_iota(jnp.int32, (8, 128), 0)
    keep_next = jnp.where(has_next, 1.0, 0.0)
    keep_prev = jnp.where(has_prev, 1.0, 0.0)
    edge_mask = jnp.where(row < 4, keep_next, keep_prev)

    def swap(j, ch):
        peer = (me + j) % 8
        lanes = pl.ds(pl.multiple_of(peer * 128, 128), 128)
        count = CUTS[ch + 1] - CUTS[ch]
        return remote(
            filt.at[pl.ds(CUTS[ch], count), :, lanes],
            field.at[pl.ds(32 * me + CUTS[ch], count)],
            swap_send.at[j - 1, ch], swap_recv.at[j - 1, ch], dom, peer,
        )

    for ch in range(CHUNKS):
        pl.when(has_prev)(lambda: to_next(ch).wait_recv())
        pl.when(has_next)(lambda: to_prev(ch).wait_recv())

        def one_band(b, carry):
            new = filter_band(
                columns(orb, (b,)), columns(prv, (b,)), columns(nxt, (b,)),
                columns(pot), columns(pot_edge), centre_of[pl.ds(b, 1), :], edge_mask,
            )
            for c in range(8):
                filt[b, :, 128 * c : 128 * c + 128] = new[c]
            return carry

        lax.fori_loop(CUTS[ch], CUTS[ch + 1], one_band, 0)
        for j in range(1, 8):
            swap(j, ch).start()

    mine = pl.ds(pl.multiple_of(me * 128, 128), 128)
    field[pl.ds(32 * me, 32)] = filt[:, :, mine]
    pl.semaphore_wait(hello, 2)
    for ch in range(CHUNKS):
        for j in range(1, 8):
            swap(j, ch).wait_recv()

    total_gram = None
    for k in range(0, 8, 2):
        part = jnp.concatenate([field[:, k, :], field[:, k + 1, :]], axis=1)
        dense[:, 128 * k : 128 * k + 256] = part
        term = nt_dot(part, part)
        total_gram = term if total_gram is None else total_gram + term
    local[...] = total_gram

    def rs(j):
        peer = (me + j) % 8
        return remote(
            local.at[pl.ds(pl.multiple_of(32 * peer, 32), 32)], band_in.at[me],
            rs_send.at[j - 1], rs_recv.at[j - 1], dom, peer,
        )

    for j in range(1, 8):
        rs(j).start()
    band_in[me] = local[pl.ds(pl.multiple_of(32 * me, 32), 32), :]
    for j in range(1, 8):
        rs(j).wait_recv()
    acc = band_in[0]
    for k in range(1, 8):
        acc = acc + band_in[k]
    for k in range(8):
        share[k] = acc[8 * (k // 2) : 8 * (k // 2) + 8, 128 * (k % 2) : 128 * (k % 2) + 128]

    def zsum(j):
        peer = (z + j) % ZS
        return remote(share.at[peer], zsum_in.at[z], z_send.at[j - 1], z_recv.at[j - 1], x * ZS + peer, me)

    for j in range(1, ZS):
        zsum(j).start()
    zsum_in[z] = share[z]
    for j in range(1, ZS):
        zsum(j).wait_recv()
    acc = zsum_in[0]
    for k in range(1, ZS):
        acc = acc + zsum_in[k]
    parts_in[x, z] = acc

    def spread_part(dx, dz):
        here = parts_in.at[x, z]
        return remote(
            here, here, part_send.at[dx, dz], part_recv.at[dx, dz],
            ((x + dx) % XS) * ZS + (z + dz) % ZS, me,
        )

    others = [(dx, dz) for dz in (4, 3, 5, 2, 6, 1, 7, 0) for dx in (2, 1, 3, 0) if dx or dz]
    for dx, dz in others:
        spread_part(dx, dz).start()
    for dx, dz in others:
        spread_part(dx, dz).wait_recv()
    for k in range(ZS):
        acc = parts_in[0, k]
        for i in range(1, XS):
            acc = acc + parts_in[i, k]
        m[
            pl.ds(pl.multiple_of(32 * me + 8 * (k // 2), 8), 8), 128 * (k % 2) : 128 * (k % 2) + 128
        ] = acc * (1.0 / (256 * 1024))

    def bgather(j, half):
        here = m.at[pl.ds(pl.multiple_of(32 * me, 32), 32), pl.ds(128 * half, 128)]
        return remote(here, here, g_send.at[half, j - 1], g_recv.at[half, j - 1], dom, (me + j) % 8)

    for half in range(2):
        for j in range(1, 8):
            bgather(j, half).start()
    factor[...] = jnp.zeros((256, 256), F32)

    def first_block_here():
        for j in range(1, 8):
            pl.when((me - j + 8) % 8 < 2)(lambda: bgather(j, 0).wait_recv())

    def whole_gram_here():
        for j in range(1, 8):
            pl.when((me - j + 8) % 8 >= 2)(lambda: bgather(j, 0).wait_recv())
            bgather(j, 1).wait_recv()
            bgather(j, 0).wait_send()
            bgather(j, 1).wait_send()

    def give(d):
        j = (d - me + 8) % 8
        return remote(
            rows.at[pl.ds(32 * d, 32)], out.at[:, :, mine], give_send.at[j], give_recv.at[j], dom, d
        )

    n = 256
    first_block_here()
    for blk in range(n // BLOCK):
        lo, hi = blk * BLOCK, (blk + 1) * BLOCK
        base = lo // 128 * 128
        diag = []
        for i in range(BLOCK // 8):
            d = m[lo + 8 * i : lo + 8 * i + 8, base : base + 128]
            if lo != base:
                d = pltpu.roll(d, 128 - (lo - base), 1)
            diag.append(d)
        rest = dense[lo:hi, :]
        if lo:
            rest = rest - nn_dot(lower[lo:hi, :lo], done[:lo, :])
        both = eliminate(diag)
        if not blk:
            whole_gram_here()
        for i in range(BLOCK // 8):
            duo[8 * i : 8 * i + 8, :] = both[i]
        r_jj, w_jj = duo[:, :BLOCK], duo[:, BLOCK:]
        factor[lo:hi, lo:hi] = r_jj
        if hi < n:
            new = nn_dot(w_jj, m[lo:hi, :])[:, hi:]
            factor[lo:hi, hi:] = new
            left = nt_dot(m[hi:, lo:hi], w_jj)
            lower[hi:, lo:hi] = left
            m[hi:, hi:] = m[hi:, hi:] - nn_dot(left, new)
        parts = 1 if hi < n else 2
        for part in range(parts):
            top, count = part * BLOCK // parts, BLOCK // parts
            solved = nn_dot(w_jj[top : top + count], rest)
            if hi < n:
                done[lo:hi, :] = solved
            for k in range(8):
                rows[lo + top : lo + top + count, k, :] = solved[:, 128 * k : 128 * k + 128]
            for d in range((lo + top) // 32, (lo + top + count) // 32):
                pl.when(me != d)(lambda: give(d).start())

    out[:, :, mine] = rows[pl.ds(32 * me, 32)]

    pl.when(has_next)(lambda: seed_next().wait_send())
    pl.when(has_prev)(lambda: seed_prev().wait_send())
    for ch in range(CHUNKS):
        pl.when(has_next)(lambda: to_next(ch).wait_send())
        pl.when(has_prev)(lambda: to_prev(ch).wait_send())
        for j in range(1, 8):
            swap(j, ch).wait_send()
    for j in range(1, 8):
        rs(j).wait_send()
    for j in range(1, ZS):
        zsum(j).wait_send()
    for dx, dz in others:
        spread_part(dx, dz).wait_send()
    for d in range(8):
        pl.when(me != d)(lambda: give(d).wait_send())
    for j in range(1, 8):
        remote(
            rows.at[pl.ds(0, 32)], out.at[:, :, mine], give_send.at[j], give_recv.at[j], dom, (me + j) % 8
        ).wait_recv()


def step_call(orb, seed, levels, sizes, centres):
    dma = pltpu.SemaphoreType.DMA
    vmem = pltpu.VMEM
    block = vmem((32, 8, 1024), F32)
    plane = vmem((8, 1024), F32)
    square = vmem((256, 256), F32)
    hbm = pl.BlockSpec(memory_space=pltpu.MemorySpace.HBM)
    return pl.pallas_call(
        step_kernel,
        out_shape=(
            jax.ShapeDtypeStruct((32, 8, 1024), F32),
            jax.ShapeDtypeStruct((256, 256), F32),
        ),
        in_specs=[hbm] * 5,
        out_specs=(VM, VM),
        scratch_shapes=[
            pltpu.SMEM((16,), F32), pltpu.SMEM((16,), jnp.int32), pltpu.SMEM((16,), F32),
            block, vmem((8, 1024), jnp.int32), block, block, vmem((8, 1024), jnp.int32),
            plane, plane, vmem((32, 128), F32), block,
            vmem((256, 8, 128), F32), vmem((256, 1024), F32), square, vmem((8, 32, 256), F32),
            vmem((8, 8, 128), F32), vmem((ZS, 8, 128), F32), vmem((XS, ZS, 8, 128), F32),
            square, square, vmem((BLOCK, 128), F32), vmem((256, 1024), F32), vmem((256, 8, 128), F32),
            dma((5,)), pltpu.SemaphoreType.REGULAR,
            dma((2, CHUNKS)), dma((2, CHUNKS)), dma((2,)), dma((2,)),
            dma((7, CHUNKS)), dma((7, CHUNKS)),
            dma((7,)), dma((7,)), dma((7,)), dma((7,)), dma((XS, ZS)), dma((XS, ZS)),
            dma((2, 7)), dma((2, 7)), dma((8,)), dma((8,)),
        ],
        compiler_params=pltpu.CompilerParams(
            collective_id=0, has_side_effects=True, vmem_limit_bytes=24 << 20
        ),
        name="filtered_step",
    )(*(pltpu.with_memory_space_constraint(a, pltpu.HBM) for a in (orb, seed, levels, sizes, centres)))


def finish_kernel(out, factor, out_h, factor_h, sem):
    copies = [
        pltpu.make_async_copy(out, out_h, sem.at[0]),
        pltpu.make_async_copy(factor, factor_h, sem.at[1]),
    ]
    for copy in copies:
        copy.start()
    for copy in copies:
        copy.wait()


def finish_call(out, factor):
    hbm = pl.BlockSpec(memory_space=pl.ANY)
    return pl.pallas_call(
        finish_kernel,
        out_shape=(
            jax.ShapeDtypeStruct((32, 8, 1024), F32),
            jax.ShapeDtypeStruct((256, 256), F32),
        ),
        in_specs=[VM, VM],
        out_specs=(hbm, hbm),
        scratch_shapes=[pltpu.SemaphoreType.DMA((2,))],
        compiler_params=pltpu.CompilerParams(vmem_limit_bytes=4 << 20),
        name="write_results",
    )(out, factor)


def shards(orbitals, seed_index, levels, group_sizes, centres):
    return finish_call(*step_call(orbitals, seed_index, levels, group_sizes, centres))


def solution(mesh):
    in_specs = (P("band", "domain", None), P("domain", None), P(), P(), P())
    out_specs = (P("band", "domain", None), P())
    return jax.shard_map(
        shards, mesh=mesh, in_specs=in_specs, out_specs=out_specs, check_vma=False
    )
```

```python
import functools

import jax
import jax.numpy as jnp
from jax import lax
from jax.experimental import pallas as pl
from jax.experimental.pallas import tpu as pltpu
from jax.sharding import PartitionSpec as P

F32 = jnp.float32
MESH = pl.DeviceIdType.MESH
VM = pl.BlockSpec(memory_space=pltpu.VMEM)
SM = pl.BlockSpec(memory_space=pltpu.SMEM)
HIGHEST = lax.Precision.HIGHEST

WEIGHTS = (-205.0 / 72.0, 8.0 / 5.0, -1.0 / 5.0, 8.0 / 315.0, -1.0 / 560.0)
SCALED = tuple(-0.5 / 5.0 * w for w in WEIGHTS)
CUTS = (0, 8, 16, 24, 28, 30, 32)
CHUNKS = len(CUTS) - 1
FAR = (4, 5, 3, 2, 6, 1, 7)
BLOCK = 64
PANEL = 16
XS, ZS = 4, 8


def remote(src, dst, send, recv, domain, band):
    return pltpu.make_async_remote_copy(
        src_ref=src, dst_ref=dst, send_sem=send, recv_sem=recv,
        device_id=(domain, band), device_id_type=MESH,
    )


def nt_dot(a, b):
    return lax.dot_general(
        a, b, (((1,), (1,)), ((), ())), precision=HIGHEST, preferred_element_type=F32
    )


def nn_dot(a, b):
    return jnp.dot(a, b, precision=HIGHEST, preferred_element_type=F32)


def up(v, r):
    return pltpu.roll(v, 8 - r, 0)


def down(v, r):
    return pltpu.roll(v, r, 0)


def plane_part(v, weights):
    lane = lax.broadcasted_iota(jnp.int32, (8, 128), 1)
    y = lane % 32
    w = weights
    zero = jnp.zeros((8, 128), F32)
    turned = {k: [pltpu.roll(c, 128 - 32 * k, 1) for c in v] for k in (1, 2, 3)}
    out = []
    for c in range(8):
        def beside(k):
            nxt = turned[k][c + 1] if c < 7 else zero
            prv = turned[k][c - 1] if c > 0 else zero
            return jnp.where(lane >= 128 - 32 * k, nxt, prv)

        s = w[2] * (turned[2][c] + beside(2))
        s += jnp.where(lane < 96, w[1], w[3]) * turned[1][c]
        s += jnp.where(lane >= 96, w[1], w[3]) * beside(1)
        s += jnp.where(lane < 32, w[3], w[1]) * turned[3][c]
        s += jnp.where(lane >= 32, w[3], w[1]) * beside(3)
        far = (v[c + 1] if c < 7 else zero) + (v[c - 1] if c > 0 else zero)
        s += w[4] * far
        for r in range(1, 5):
            s += jnp.where(y + r < 32, w[r], 0.0) * pltpu.roll(v[c], 128 - r, 1)
            s += jnp.where(y - r >= 0, w[r], 0.0) * pltpu.roll(v[c], r, 1)
        out.append(s)
    return out


def filter_band(own, prv, nxt, pot_own, pot_edge, centre, edge_mask):
    w = SCALED
    row = lax.broadcasted_iota(jnp.int32, (8, 128), 0)
    edge = [jnp.where(row < 4, n, p) for n, p in zip(nxt, prv)]
    flat_own = plane_part(own, w)
    flat_edge = plane_part(edge, w)
    one_own, one_edge = [], []
    for c in range(8):
        o, p, n, e = own[c], prv[c], nxt[c], edge[c]
        s = flat_own[c]
        t = flat_edge[c]
        for r in range(1, 4):
            above = up(jnp.where(row >= r, o, n), r)
            below = down(jnp.where(row < 8 - r, o, p), r)
            s += w[r] * (above + below)
            above = up(jnp.where(row < r, o, jnp.where(row < r + 4, n, p)), r)
            below = down(jnp.where(row >= 8 - r, o, jnp.where(row < 4 - r, n, p)), r)
            t += w[r] * (above + below)
        s += w[4] * down(jnp.where(row >= 4, o, n) + jnp.where(row < 4, o, p), 4)
        t += w[4] * down(jnp.where(row < 4, o, n) + jnp.where(row >= 4, o, p), 4)
        s += (3.0 * w[0] + 0.2 * (pot_own[c] - centre)) * o
        t += (3.0 * w[0] + 0.2 * (pot_edge[c] - centre)) * e
        one_own.append(s)
        one_edge.append(t * edge_mask)
    flat = plane_part(one_own, w)
    out = []
    for c in range(8):
        o, e = one_own[c], one_edge[c]
        s = flat[c]
        for r in range(1, 4):
            above = up(jnp.where(row >= r, o, e), r)
            below = down(jnp.where(row < 8 - r, o, e), r)
            s += w[r] * (above + below)
        s += w[4] * down(o + e, 4)
        s += (3.0 * w[0] + 0.2 * (pot_own[c] - centre)) * o
        out.append(2.0 * s - own[c])
    return out


def columns(ref, lead=()):
    return [ref[(*lead, slice(None), slice(128 * c, 128 * c + 128))] for c in range(8)]


def eliminate(diag):
    row = lax.broadcasted_iota(jnp.int32, (8, 128), 0)
    lane = lax.broadcasted_iota(jnp.int32, (8, 128), 1)
    groups = BLOCK // 8
    a = []
    for i in range(groups):
        unit = jnp.where(lane == row + (BLOCK + 8 * i), 1.0, 0.0)
        a.append(jnp.where(lane < BLOCK, diag[i], unit))
    step = PANEL // 8
    for p in range(0, groups, step):
        spread = [
            [jnp.broadcast_to(a[i][:, 8 * p + l : 8 * p + l + 1], (8, 128)) for i in range(p, groups)]
            for l in range(PANEL)
        ]
        for k in range(PANEL):
            g, at = k // 8, k % 8
            first = spread[k][g]
            inv = 1.0 / first[at : at + 1, :]
            mult = [jnp.where(row > at, first, 0.0)] + spread[k][g + 1 :]
            for l in range(k + 1, PANEL):
                t = spread[l][g][at : at + 1, :] * inv
                spread[l] = spread[l][:g] + [v - m * t for v, m in zip(spread[l][g:], mult)]
            pivot_row = a[p + g][at : at + 1, :] * inv
            for i in range(p + g, groups):
                a[i] = a[i] - mult[i - p - g] * pivot_row
    out = []
    for i in range(groups):
        d = jnp.sum(jnp.where(lane == row + 8 * i, a[i], 0.0), axis=1, keepdims=True)
        scaled = a[i] * lax.rsqrt(d)
        out.append(jnp.where(jnp.logical_or(lane >= BLOCK, lane >= row + 8 * i), scaled, 0.0))
    return out

def step_kernel(
    orb_h, seed_h, levels_h, sizes_h, centres_h,
    out, factor,
    levels, sizes, centres, orb, seed, prv, nxt, seed_edge, pot, pot_edge, centre_of, filt,
    field, dense, local, band_in, share, zsum_in, parts_in, m, lower, duo, done, rows,
    in_sem, hello, halo_send, halo_recv, seed_send, seed_recv, swap_send, swap_recv,
    rs_send, rs_recv, z_send, z_recv, part_send, part_recv, g_send, g_recv,
    give_send, give_recv,
):
    dom, me = lax.axis_index("domain"), lax.axis_index("band")
    x, z = dom // ZS, dom % ZS
    has_prev, has_next = dom > 0, dom < XS * ZS - 1

    barrier = pltpu.get_barrier_semaphore()

    def greet(d, b):
        pl.semaphore_signal(barrier, inc=1, device_id=(d, b), device_id_type=MESH)

    outer_prev = jnp.logical_and(has_prev, z == 0)
    outer_next = jnp.logical_and(has_next, z == ZS - 1)
    pl.when(outer_prev)(lambda: greet(dom - 1, me))
    pl.when(outer_next)(lambda: greet(dom + 1, me))
    for j in (1, 7, 2, 6):
        greet(x * ZS + (z + j) % ZS, me)
    for j in range(1, 8):
        greet(dom, (me + j) % 8)
    for j in range(1, XS):
        greet(((x + j) % XS) * ZS + z, me)

    loads = [
        pltpu.make_async_copy(levels_h, levels, in_sem.at[0]),
        pltpu.make_async_copy(sizes_h, sizes, in_sem.at[1]),
        pltpu.make_async_copy(centres_h, centres, in_sem.at[2]),
        pltpu.make_async_copy(seed_h, seed, in_sem.at[3]),
        pltpu.make_async_copy(orb_h, orb, in_sem.at[4]),
    ]
    for load in loads:
        load.start()

    @pl.when(jnp.logical_not(has_prev))
    def _():
        prv[...] = jnp.zeros_like(prv)
        seed_edge[4:8, :] = jnp.zeros((4, 1024), jnp.int32)

    @pl.when(jnp.logical_not(has_next))
    def _():
        nxt[...] = jnp.zeros_like(nxt)
        seed_edge[0:4, :] = jnp.zeros((4, 1024), jnp.int32)

    one = jnp.int32(1)
    pl.semaphore_wait(barrier, 14 + jnp.where(outer_prev, one, 0) + jnp.where(outer_next, one, 0))

    def to_next(ch):
        part = pl.ds(CUTS[ch], CUTS[ch + 1] - CUTS[ch])
        return remote(orb_h.at[part], prv.at[part], halo_send.at[0, ch], halo_recv.at[0, ch], dom + 1, me)

    def to_prev(ch):
        part = pl.ds(CUTS[ch], CUTS[ch + 1] - CUTS[ch])
        return remote(orb_h.at[part], nxt.at[part], halo_send.at[1, ch], halo_recv.at[1, ch], dom - 1, me)

    def seed_next():
        return remote(seed.at[pl.ds(4, 4)], seed_edge.at[pl.ds(4, 4)], seed_send.at[0], seed_recv.at[0], dom + 1, me)

    def seed_prev():
        return remote(seed.at[pl.ds(0, 4)], seed_edge.at[pl.ds(0, 4)], seed_send.at[1], seed_recv.at[1], dom - 1, me)

    loads[3].wait()

    @pl.when(has_next)
    def _():
        seed_next().start()
        for ch in range(CHUNKS):
            to_next(ch).start()

    @pl.when(has_prev)
    def _():
        seed_prev().start()
        for ch in range(CHUNKS):
            to_prev(ch).start()

    for j in (2, 6):
        pl.semaphore_signal(hello, inc=1, device_id=(x * ZS + (z + j) % ZS, me), device_id_type=MESH)

    for load in loads[:3] + loads[4:]:
        load.wait()

    def lookup(index):
        value = jnp.zeros(index.shape, F32)
        for t in range(16):
            value = jnp.where(index == t, levels[t], value)
        return value

    pot[...] = lookup(seed[...])
    band = lax.broadcasted_iota(jnp.int32, (32, 128), 0) + 32 * me
    total = sizes[0]
    value = jnp.full((32, 128), centres[0], F32)
    for g in range(15):
        value = jnp.where(total <= band, centres[g + 1], value)
        total = total + sizes[g + 1]
    centre_of[...] = value

    pl.when(has_prev)(lambda: seed_next().wait_recv())
    pl.when(has_next)(lambda: seed_prev().wait_recv())
    pot_edge[...] = lookup(seed_edge[...])

    row = lax.broadcasted_iota(jnp.int32, (8, 128), 0)
    keep_next = jnp.where(has_next, 1.0, 0.0)
    keep_prev = jnp.where(has_prev, 1.0, 0.0)
    edge_mask = jnp.where(row < 4, keep_next, keep_prev)

    def swap(j, ch):
        peer = (me + j) % 8
        lanes = pl.ds(pl.multiple_of(peer * 128, 128), 128)
        count = CUTS[ch + 1] - CUTS[ch]
        return remote(
            filt.at[pl.ds(CUTS[ch], count), :, lanes],
            field.at[pl.ds(32 * me + CUTS[ch], count)],
            swap_send.at[j - 1, ch], swap_recv.at[j - 1, ch], dom, peer,
        )

    for ch in range(CHUNKS):
        pl.when(has_prev)(lambda: to_next(ch).wait_recv())
        pl.when(has_next)(lambda: to_prev(ch).wait_recv())

        def one_band(b, carry):
            new = filter_band(
                columns(orb, (b,)), columns(prv, (b,)), columns(nxt, (b,)),
                columns(pot), columns(pot_edge), centre_of[pl.ds(b, 1), :], edge_mask,
            )
            for c in range(8):
                filt[b, :, 128 * c : 128 * c + 128] = new[c]
            return carry

        lax.fori_loop(CUTS[ch], CUTS[ch + 1], one_band, 0)
        for j in FAR:
            swap(j, ch).start()

    mine = pl.ds(pl.multiple_of(me * 128, 128), 128)
    field[pl.ds(32 * me, 32)] = filt[:, :, mine]
    pl.semaphore_wait(hello, 2)
    for ch in range(CHUNKS):
        for j in range(1, 8):
            swap(j, ch).wait_recv()

    total_gram = None
    for k in range(0, 8, 2):
        part = jnp.concatenate([field[:, k, :], field[:, k + 1, :]], axis=1)
        dense[:, 128 * k : 128 * k + 256] = part
        term = nt_dot(part, part)
        total_gram = term if total_gram is None else total_gram + term
    local[...] = total_gram

    def rs(j):
        peer = (me + j) % 8
        return remote(
            local.at[pl.ds(pl.multiple_of(32 * peer, 32), 32)], band_in.at[me],
            rs_send.at[j - 1], rs_recv.at[j - 1], dom, peer,
        )

    for j in FAR:
        rs(j).start()
    band_in[me] = local[pl.ds(pl.multiple_of(32 * me, 32), 32), :]
    for j in range(1, 8):
        rs(j).wait_recv()
    acc = band_in[0]
    for k in range(1, 8):
        acc = acc + band_in[k]
    for k in range(8):
        share[k] = acc[8 * (k // 2) : 8 * (k // 2) + 8, 128 * (k % 2) : 128 * (k % 2) + 128]

    def zsum(j):
        peer = (z + j) % ZS
        return remote(share.at[peer], zsum_in.at[z], z_send.at[j - 1], z_recv.at[j - 1], x * ZS + peer, me)

    for j in FAR:
        zsum(j).start()
    zsum_in[z] = share[z]
    for j in range(1, ZS):
        zsum(j).wait_recv()
    acc = zsum_in[0]
    for k in range(1, ZS):
        acc = acc + zsum_in[k]
    parts_in[x, z] = acc

    def spread_part(dx, dz):
        here = parts_in.at[x, z]
        return remote(
            here, here, part_send.at[dx, dz], part_recv.at[dx, dz],
            ((x + dx) % XS) * ZS + (z + dz) % ZS, me,
        )

    others = [(dx, dz) for dz in (4, 3, 5, 2, 6, 1, 7, 0) for dx in (2, 1, 3, 0) if dx or dz]
    for dx, dz in others:
        spread_part(dx, dz).start()
    for dx, dz in others:
        spread_part(dx, dz).wait_recv()
    for k in range(ZS):
        acc = parts_in[0, k]
        for i in range(1, XS):
            acc = acc + parts_in[i, k]
        m[
            pl.ds(pl.multiple_of(32 * me + 8 * (k // 2), 8), 8), 128 * (k % 2) : 128 * (k % 2) + 128
        ] = acc * (1.0 / (256 * 1024))

    def bgather(j, half):
        here = m.at[pl.ds(pl.multiple_of(32 * me, 32), 32), pl.ds(128 * half, 128)]
        return remote(here, here, g_send.at[half, j - 1], g_recv.at[half, j - 1], dom, (me + j) % 8)

    for half in range(2):
        for j in FAR:
            bgather(j, half).start()
    factor[...] = jnp.zeros((256, 256), F32)

    def first_block_here():
        for j in range(1, 8):
            pl.when((me - j + 8) % 8 < 2)(lambda: bgather(j, 0).wait_recv())

    def whole_gram_here():
        for j in range(1, 8):
            pl.when((me - j + 8) % 8 >= 2)(lambda: bgather(j, 0).wait_recv())
            bgather(j, 1).wait_recv()
            bgather(j, 0).wait_send()
            bgather(j, 1).wait_send()

    def give(d):
        j = (d - me + 8) % 8
        return remote(
            rows.at[pl.ds(32 * d, 32)], out.at[:, :, mine], give_send.at[j], give_recv.at[j], dom, d
        )

    n = 256
    first_block_here()
    for blk in range(n // BLOCK):
        lo, hi = blk * BLOCK, (blk + 1) * BLOCK
        base = lo // 128 * 128
        diag = []
        for i in range(BLOCK // 8):
            d = m[lo + 8 * i : lo + 8 * i + 8, base : base + 128]
            if lo != base:
                d = pltpu.roll(d, 128 - (lo - base), 1)
            diag.append(d)
        rest = dense[lo:hi, :]
        if lo:
            rest = rest - nn_dot(lower[lo:hi, :lo], done[:lo, :])
        both = eliminate(diag)
        if not blk:
            whole_gram_here()
        for i in range(BLOCK // 8):
            duo[8 * i : 8 * i + 8, :] = both[i]
        r_jj, w_jj = duo[:, :BLOCK], duo[:, BLOCK:]
        factor[lo:hi, lo:hi] = r_jj
        if hi < n:
            new = nn_dot(w_jj, m[lo:hi, :])[:, hi:]
            factor[lo:hi, hi:] = new
            left = nt_dot(m[hi:, lo:hi], w_jj)
            lower[hi:, lo:hi] = left
            m[hi:, hi:] = m[hi:, hi:] - nn_dot(left, new)
        parts = 1 if hi < n else 2
        for part in range(parts):
            top, count = part * BLOCK // parts, BLOCK // parts
            solved = nn_dot(w_jj[top : top + count], rest)
            if hi < n:
                done[lo:hi, :] = solved
            for k in range(8):
                rows[lo + top : lo + top + count, k, :] = solved[:, 128 * k : 128 * k + 128]
            for d in range((lo + top) // 32, (lo + top + count) // 32):
                pl.when(me != d)(lambda: give(d).start())

    out[:, :, mine] = rows[pl.ds(32 * me, 32)]

    pl.when(has_next)(lambda: seed_next().wait_send())
    pl.when(has_prev)(lambda: seed_prev().wait_send())
    for ch in range(CHUNKS):
        pl.when(has_next)(lambda: to_next(ch).wait_send())
        pl.when(has_prev)(lambda: to_prev(ch).wait_send())
        for j in range(1, 8):
            swap(j, ch).wait_send()
    for j in range(1, 8):
        rs(j).wait_send()
    for j in range(1, ZS):
        zsum(j).wait_send()
    for dx, dz in others:
        spread_part(dx, dz).wait_send()
    for d in range(8):
        pl.when(me != d)(lambda: give(d).wait_send())
    for j in range(1, 8):
        remote(
            rows.at[pl.ds(0, 32)], out.at[:, :, mine], give_send.at[j], give_recv.at[j], dom, (me + j) % 8
        ).wait_recv()


def step_call(orb, seed, levels, sizes, centres):
    dma = pltpu.SemaphoreType.DMA
    vmem = pltpu.VMEM
    block = vmem((32, 8, 1024), F32)
    plane = vmem((8, 1024), F32)
    square = vmem((256, 256), F32)
    hbm = pl.BlockSpec(memory_space=pltpu.MemorySpace.HBM)
    return pl.pallas_call(
        step_kernel,
        out_shape=(
            jax.ShapeDtypeStruct((32, 8, 1024), F32),
            jax.ShapeDtypeStruct((256, 256), F32),
        ),
        in_specs=[hbm] * 5,
        out_specs=(VM, VM),
        scratch_shapes=[
            pltpu.SMEM((16,), F32), pltpu.SMEM((16,), jnp.int32), pltpu.SMEM((16,), F32),
            block, vmem((8, 1024), jnp.int32), block, block, vmem((8, 1024), jnp.int32),
            plane, plane, vmem((32, 128), F32), block,
            vmem((256, 8, 128), F32), vmem((256, 1024), F32), square, vmem((8, 32, 256), F32),
            vmem((8, 8, 128), F32), vmem((ZS, 8, 128), F32), vmem((XS, ZS, 8, 128), F32),
            square, square, vmem((BLOCK, 128), F32), vmem((256, 1024), F32), vmem((256, 8, 128), F32),
            dma((5,)), pltpu.SemaphoreType.REGULAR,
            dma((2, CHUNKS)), dma((2, CHUNKS)), dma((2,)), dma((2,)),
            dma((7, CHUNKS)), dma((7, CHUNKS)),
            dma((7,)), dma((7,)), dma((7,)), dma((7,)), dma((XS, ZS)), dma((XS, ZS)),
            dma((2, 7)), dma((2, 7)), dma((8,)), dma((8,)),
        ],
        compiler_params=pltpu.CompilerParams(
            collective_id=0, has_side_effects=True, vmem_limit_bytes=24 << 20
        ),
        name="filtered_step",
    )(*(pltpu.with_memory_space_constraint(a, pltpu.HBM) for a in (orb, seed, levels, sizes, centres)))


def finish_kernel(out, factor, out_h, factor_h, sem):
    copies = [
        pltpu.make_async_copy(out, out_h, sem.at[0]),
        pltpu.make_async_copy(factor, factor_h, sem.at[1]),
    ]
    for copy in copies:
        copy.start()
    for copy in copies:
        copy.wait()


def finish_call(out, factor):
    hbm = pl.BlockSpec(memory_space=pl.ANY)
    return pl.pallas_call(
        finish_kernel,
        out_shape=(
            jax.ShapeDtypeStruct((32, 8, 1024), F32),
            jax.ShapeDtypeStruct((256, 256), F32),
        ),
        in_specs=[VM, VM],
        out_specs=(hbm, hbm),
        scratch_shapes=[pltpu.SemaphoreType.DMA((2,))],
        compiler_params=pltpu.CompilerParams(vmem_limit_bytes=4 << 20),
        name="write_results",
    )(out, factor)


def shards(orbitals, seed_index, levels, group_sizes, centres):
    return finish_call(*step_call(orbitals, seed_index, levels, group_sizes, centres))


def solution(mesh):
    in_specs = (P("band", "domain", None), P("domain", None), P(), P(), P())
    out_specs = (P("band", "domain", None), P())
    return jax.shard_map(
        shards, mesh=mesh, in_specs=in_specs, out_specs=out_specs, check_vma=False
    )
```

```python
import functools

import jax
import jax.numpy as jnp
from jax import lax
from jax.experimental import pallas as pl
from jax.experimental.pallas import tpu as pltpu
from jax.sharding import PartitionSpec as P

F32 = jnp.float32
MESH = pl.DeviceIdType.MESH
VM = pl.BlockSpec(memory_space=pltpu.VMEM)
SM = pl.BlockSpec(memory_space=pltpu.SMEM)
HIGHEST = lax.Precision.HIGHEST

WEIGHTS = (-205.0 / 72.0, 8.0 / 5.0, -1.0 / 5.0, 8.0 / 315.0, -1.0 / 560.0)
SCALED = tuple(-0.5 / 5.0 * w for w in WEIGHTS)
CUTS = (0, 4, 12, 20, 27, 30, 32)
CHUNKS = len(CUTS) - 1
FAR = (4, 5, 3, 2, 6, 1, 7)
BLOCK = 64
PANEL = 16
XS, ZS = 4, 8


def remote(src, dst, send, recv, domain, band):
    return pltpu.make_async_remote_copy(
        src_ref=src, dst_ref=dst, send_sem=send, recv_sem=recv,
        device_id=(domain, band), device_id_type=MESH,
    )


def nt_dot(a, b):
    return lax.dot_general(
        a, b, (((1,), (1,)), ((), ())), precision=HIGHEST, preferred_element_type=F32
    )


def nn_dot(a, b):
    return jnp.dot(a, b, precision=HIGHEST, preferred_element_type=F32)


def up(v, r):
    return pltpu.roll(v, 8 - r, 0)


def down(v, r):
    return pltpu.roll(v, r, 0)


def plane_part(v, weights):
    lane = lax.broadcasted_iota(jnp.int32, (8, 128), 1)
    y = lane % 32
    w = weights
    zero = jnp.zeros((8, 128), F32)
    turned = {k: [pltpu.roll(c, 128 - 32 * k, 1) for c in v] for k in (1, 2, 3)}
    out = []
    for c in range(8):
        def beside(k):
            nxt = turned[k][c + 1] if c < 7 else zero
            prv = turned[k][c - 1] if c > 0 else zero
            return jnp.where(lane >= 128 - 32 * k, nxt, prv)

        s = w[2] * (turned[2][c] + beside(2))
        s += jnp.where(lane < 96, w[1], w[3]) * turned[1][c]
        s += jnp.where(lane >= 96, w[1], w[3]) * beside(1)
        s += jnp.where(lane < 32, w[3], w[1]) * turned[3][c]
        s += jnp.where(lane >= 32, w[3], w[1]) * beside(3)
        far = (v[c + 1] if c < 7 else zero) + (v[c - 1] if c > 0 else zero)
        s += w[4] * far
        for r in range(1, 5):
            s += jnp.where(y + r < 32, w[r], 0.0) * pltpu.roll(v[c], 128 - r, 1)
            s += jnp.where(y - r >= 0, w[r], 0.0) * pltpu.roll(v[c], r, 1)
        out.append(s)
    return out


def filter_band(own, prv, nxt, pot_own, pot_edge, centre, edge_mask):
    w = SCALED
    row = lax.broadcasted_iota(jnp.int32, (8, 128), 0)
    edge = [jnp.where(row < 4, n, p) for n, p in zip(nxt, prv)]
    flat_own = plane_part(own, w)
    flat_edge = plane_part(edge, w)
    one_own, one_edge = [], []
    for c in range(8):
        o, p, n, e = own[c], prv[c], nxt[c], edge[c]
        s = flat_own[c]
        t = flat_edge[c]
        for r in range(1, 4):
            above = up(jnp.where(row >= r, o, n), r)
            below = down(jnp.where(row < 8 - r, o, p), r)
            s += w[r] * (above + below)
            above = up(jnp.where(row < r, o, jnp.where(row < r + 4, n, p)), r)
            below = down(jnp.where(row >= 8 - r, o, jnp.where(row < 4 - r, n, p)), r)
            t += w[r] * (above + below)
        s += w[4] * down(jnp.where(row >= 4, o, n) + jnp.where(row < 4, o, p), 4)
        t += w[4] * down(jnp.where(row < 4, o, n) + jnp.where(row >= 4, o, p), 4)
        s += (3.0 * w[0] + 0.2 * (pot_own[c] - centre)) * o
        t += (3.0 * w[0] + 0.2 * (pot_edge[c] - centre)) * e
        one_own.append(s)
        one_edge.append(t * edge_mask)
    flat = plane_part(one_own, w)
    out = []
    for c in range(8):
        o, e = one_own[c], one_edge[c]
        s = flat[c]
        for r in range(1, 4):
            above = up(jnp.where(row >= r, o, e), r)
            below = down(jnp.where(row < 8 - r, o, e), r)
            s += w[r] * (above + below)
        s += w[4] * down(o + e, 4)
        s += (3.0 * w[0] + 0.2 * (pot_own[c] - centre)) * o
        out.append(2.0 * s - own[c])
    return out


def columns(ref, lead=()):
    return [ref[(*lead, slice(None), slice(128 * c, 128 * c + 128))] for c in range(8)]


def eliminate(diag):
    row = lax.broadcasted_iota(jnp.int32, (8, 128), 0)
    lane = lax.broadcasted_iota(jnp.int32, (8, 128), 1)
    groups = BLOCK // 8
    a = []
    for i in range(groups):
        unit = jnp.where(lane == row + (BLOCK + 8 * i), 1.0, 0.0)
        a.append(jnp.where(lane < BLOCK, diag[i], unit))
    step = PANEL // 8
    for p in range(0, groups, step):
        spread = [
            [jnp.broadcast_to(a[i][:, 8 * p + l : 8 * p + l + 1], (8, 128)) for i in range(p, groups)]
            for l in range(PANEL)
        ]
        for k in range(PANEL):
            g, at = k // 8, k % 8
            first = spread[k][g]
            inv = 1.0 / first[at : at + 1, :]
            mult = [jnp.where(row > at, first, 0.0)] + spread[k][g + 1 :]
            for l in range(k + 1, PANEL):
                t = spread[l][g][at : at + 1, :] * inv
                spread[l] = spread[l][:g] + [v - m * t for v, m in zip(spread[l][g:], mult)]
            pivot_row = a[p + g][at : at + 1, :] * inv
            for i in range(p + g, groups):
                a[i] = a[i] - mult[i - p - g] * pivot_row
    out = []
    for i in range(groups):
        d = jnp.sum(jnp.where(lane == row + 8 * i, a[i], 0.0), axis=1, keepdims=True)
        scaled = a[i] * lax.rsqrt(d)
        out.append(jnp.where(jnp.logical_or(lane >= BLOCK, lane >= row + 8 * i), scaled, 0.0))
    return out

def step_kernel(
    orb_h, seed_h, levels_h, sizes_h, centres_h,
    out, factor,
    levels, sizes, centres, orb, seed, prv, nxt, seed_edge, pot, pot_edge, centre_of, filt,
    field, dense, local, band_in, share, zsum_in, parts_in, m, lower, duo, done, rows,
    in_sem, hello, halo_send, halo_recv, seed_send, seed_recv, swap_send, swap_recv,
    rs_send, rs_recv, z_send, z_recv, part_send, part_recv, g_send, g_recv,
    give_send, give_recv,
):
    dom, me = lax.axis_index("domain"), lax.axis_index("band")
    x, z = dom // ZS, dom % ZS
    has_prev, has_next = dom > 0, dom < XS * ZS - 1

    barrier = pltpu.get_barrier_semaphore()

    def greet(d, b):
        pl.semaphore_signal(barrier, inc=1, device_id=(d, b), device_id_type=MESH)

    outer_prev = jnp.logical_and(has_prev, z == 0)
    outer_next = jnp.logical_and(has_next, z == ZS - 1)
    pl.when(outer_prev)(lambda: greet(dom - 1, me))
    pl.when(outer_next)(lambda: greet(dom + 1, me))
    for j in (1, 7, 2, 6):
        greet(x * ZS + (z + j) % ZS, me)
    for j in range(1, 8):
        greet(dom, (me + j) % 8)
    for j in range(1, XS):
        greet(((x + j) % XS) * ZS + z, me)

    loads = [
        pltpu.make_async_copy(levels_h, levels, in_sem.at[0]),
        pltpu.make_async_copy(sizes_h, sizes, in_sem.at[1]),
        pltpu.make_async_copy(centres_h, centres, in_sem.at[2]),
        pltpu.make_async_copy(seed_h, seed, in_sem.at[3]),
        pltpu.make_async_copy(orb_h, orb, in_sem.at[4]),
    ]
    for load in loads:
        load.start()

    @pl.when(jnp.logical_not(has_prev))
    def _():
        prv[...] = jnp.zeros_like(prv)
        seed_edge[4:8, :] = jnp.zeros((4, 1024), jnp.int32)

    @pl.when(jnp.logical_not(has_next))
    def _():
        nxt[...] = jnp.zeros_like(nxt)
        seed_edge[0:4, :] = jnp.zeros((4, 1024), jnp.int32)

    one = jnp.int32(1)
    pl.semaphore_wait(barrier, 14 + jnp.where(outer_prev, one, 0) + jnp.where(outer_next, one, 0))

    def to_next(ch):
        part = pl.ds(CUTS[ch], CUTS[ch + 1] - CUTS[ch])
        return remote(orb_h.at[part], prv.at[part], halo_send.at[0, ch], halo_recv.at[0, ch], dom + 1, me)

    def to_prev(ch):
        part = pl.ds(CUTS[ch], CUTS[ch + 1] - CUTS[ch])
        return remote(orb_h.at[part], nxt.at[part], halo_send.at[1, ch], halo_recv.at[1, ch], dom - 1, me)

    def seed_next():
        return remote(seed.at[pl.ds(4, 4)], seed_edge.at[pl.ds(4, 4)], seed_send.at[0], seed_recv.at[0], dom + 1, me)

    def seed_prev():
        return remote(seed.at[pl.ds(0, 4)], seed_edge.at[pl.ds(0, 4)], seed_send.at[1], seed_recv.at[1], dom - 1, me)

    loads[3].wait()

    @pl.when(has_next)
    def _():
        seed_next().start()
        for ch in range(CHUNKS):
            to_next(ch).start()

    @pl.when(has_prev)
    def _():
        seed_prev().start()
        for ch in range(CHUNKS):
            to_prev(ch).start()

    for j in (2, 6):
        pl.semaphore_signal(hello, inc=1, device_id=(x * ZS + (z + j) % ZS, me), device_id_type=MESH)

    for load in loads[:3] + loads[4:]:
        load.wait()

    def lookup(index):
        value = jnp.zeros(index.shape, F32)
        for t in range(16):
            value = jnp.where(index == t, levels[t], value)
        return value

    pot[...] = lookup(seed[...])
    band = lax.broadcasted_iota(jnp.int32, (32, 128), 0) + 32 * me
    total = sizes[0]
    value = jnp.full((32, 128), centres[0], F32)
    for g in range(15):
        value = jnp.where(total <= band, centres[g + 1], value)
        total = total + sizes[g + 1]
    centre_of[...] = value

    pl.when(has_prev)(lambda: seed_next().wait_recv())
    pl.when(has_next)(lambda: seed_prev().wait_recv())
    pot_edge[...] = lookup(seed_edge[...])

    row = lax.broadcasted_iota(jnp.int32, (8, 128), 0)
    keep_next = jnp.where(has_next, 1.0, 0.0)
    keep_prev = jnp.where(has_prev, 1.0, 0.0)
    edge_mask = jnp.where(row < 4, keep_next, keep_prev)

    def swap(j, ch):
        peer = (me + j) % 8
        lanes = pl.ds(pl.multiple_of(peer * 128, 128), 128)
        count = CUTS[ch + 1] - CUTS[ch]
        return remote(
            filt.at[pl.ds(CUTS[ch], count), :, lanes],
            field.at[pl.ds(32 * me + CUTS[ch], count)],
            swap_send.at[j - 1, ch], swap_recv.at[j - 1, ch], dom, peer,
        )

    for ch in range(CHUNKS):
        pl.when(has_prev)(lambda: to_next(ch).wait_recv())
        pl.when(has_next)(lambda: to_prev(ch).wait_recv())

        def one_band(b, carry):
            new = filter_band(
                columns(orb, (b,)), columns(prv, (b,)), columns(nxt, (b,)),
                columns(pot), columns(pot_edge), centre_of[pl.ds(b, 1), :], edge_mask,
            )
            for c in range(8):
                filt[b, :, 128 * c : 128 * c + 128] = new[c]
            return carry

        lax.fori_loop(CUTS[ch], CUTS[ch + 1], one_band, 0)
        for j in FAR:
            swap(j, ch).start()

    mine = pl.ds(pl.multiple_of(me * 128, 128), 128)
    field[pl.ds(32 * me, 32)] = filt[:, :, mine]
    pl.semaphore_wait(hello, 2)
    for ch in range(CHUNKS):
        for j in range(1, 8):
            swap(j, ch).wait_recv()

    total_gram = None
    for k in range(0, 8, 2):
        part = jnp.concatenate([field[:, k, :], field[:, k + 1, :]], axis=1)
        dense[:, 128 * k : 128 * k + 256] = part
        term = nt_dot(part, part)
        total_gram = term if total_gram is None else total_gram + term
    local[...] = total_gram

    def rs(j):
        peer = (me + j) % 8
        return remote(
            local.at[pl.ds(pl.multiple_of(32 * peer, 32), 32)], band_in.at[me],
            rs_send.at[j - 1], rs_recv.at[j - 1], dom, peer,
        )

    for j in FAR:
        rs(j).start()
    band_in[me] = local[pl.ds(pl.multiple_of(32 * me, 32), 32), :]
    for j in range(1, 8):
        rs(j).wait_recv()
    acc = band_in[0]
    for k in range(1, 8):
        acc = acc + band_in[k]
    for k in range(8):
        share[k] = acc[8 * (k // 2) : 8 * (k // 2) + 8, 128 * (k % 2) : 128 * (k % 2) + 128]

    def zsum(j):
        peer = (z + j) % ZS
        return remote(share.at[peer], zsum_in.at[z], z_send.at[j - 1], z_recv.at[j - 1], x * ZS + peer, me)

    for j in FAR:
        zsum(j).start()
    zsum_in[z] = share[z]
    for j in range(1, ZS):
        zsum(j).wait_recv()
    acc = zsum_in[0]
    for k in range(1, ZS):
        acc = acc + zsum_in[k]
    parts_in[x, z] = acc

    def spread_part(dx, dz):
        here = parts_in.at[x, z]
        return remote(
            here, here, part_send.at[dx, dz], part_recv.at[dx, dz],
            ((x + dx) % XS) * ZS + (z + dz) % ZS, me,
        )

    others = [(dx, dz) for dz in (4, 3, 5, 2, 6, 1, 7, 0) for dx in (2, 1, 3, 0) if dx or dz]
    for dx, dz in others:
        spread_part(dx, dz).start()
    for dx, dz in others:
        spread_part(dx, dz).wait_recv()
    for k in range(ZS):
        acc = parts_in[0, k]
        for i in range(1, XS):
            acc = acc + parts_in[i, k]
        m[
            pl.ds(pl.multiple_of(32 * me + 8 * (k // 2), 8), 8), 128 * (k % 2) : 128 * (k % 2) + 128
        ] = acc * (1.0 / (256 * 1024))

    def bgather(j, half):
        here = m.at[pl.ds(pl.multiple_of(32 * me, 32), 32), pl.ds(128 * half, 128)]
        return remote(here, here, g_send.at[half, j - 1], g_recv.at[half, j - 1], dom, (me + j) % 8)

    for half in range(2):
        for j in FAR:
            bgather(j, half).start()
    factor[...] = jnp.zeros((256, 256), F32)

    def first_block_here():
        for j in range(1, 8):
            pl.when((me - j + 8) % 8 < 2)(lambda: bgather(j, 0).wait_recv())

    def whole_gram_here():
        for j in range(1, 8):
            pl.when((me - j + 8) % 8 >= 2)(lambda: bgather(j, 0).wait_recv())
            bgather(j, 1).wait_recv()
            bgather(j, 0).wait_send()
            bgather(j, 1).wait_send()

    def give(d):
        j = (d - me + 8) % 8
        return remote(
            rows.at[pl.ds(32 * d, 32)], out.at[:, :, mine], give_send.at[j], give_recv.at[j], dom, d
        )

    n = 256
    first_block_here()
    for blk in range(n // BLOCK):
        lo, hi = blk * BLOCK, (blk + 1) * BLOCK
        base = lo // 128 * 128
        diag = []
        for i in range(BLOCK // 8):
            d = m[lo + 8 * i : lo + 8 * i + 8, base : base + 128]
            if lo != base:
                d = pltpu.roll(d, 128 - (lo - base), 1)
            diag.append(d)
        rest = dense[lo:hi, :]
        if lo:
            rest = rest - nn_dot(lower[lo:hi, :lo], done[:lo, :])
        both = eliminate(diag)
        if not blk:
            whole_gram_here()
        for i in range(BLOCK // 8):
            duo[8 * i : 8 * i + 8, :] = both[i]
        r_jj, w_jj = duo[:, :BLOCK], duo[:, BLOCK:]
        factor[lo:hi, lo:hi] = r_jj
        if hi < n:
            new = nn_dot(w_jj, m[lo:hi, :])[:, hi:]
            factor[lo:hi, hi:] = new
            left = nt_dot(m[hi:, lo:hi], w_jj)
            lower[hi:, lo:hi] = left
            m[hi:, hi:] = m[hi:, hi:] - nn_dot(left, new)
        parts = 1 if hi < n else 2
        for part in range(parts):
            top, count = part * BLOCK // parts, BLOCK // parts
            solved = nn_dot(w_jj[top : top + count], rest)
            if hi < n:
                done[lo:hi, :] = solved
            for k in range(8):
                rows[lo + top : lo + top + count, k, :] = solved[:, 128 * k : 128 * k + 128]
            for d in range((lo + top) // 32, (lo + top + count) // 32):
                pl.when(me != d)(lambda: give(d).start())

    out[:, :, mine] = rows[pl.ds(32 * me, 32)]

    pl.when(has_next)(lambda: seed_next().wait_send())
    pl.when(has_prev)(lambda: seed_prev().wait_send())
    for ch in range(CHUNKS):
        pl.when(has_next)(lambda: to_next(ch).wait_send())
        pl.when(has_prev)(lambda: to_prev(ch).wait_send())
        for j in range(1, 8):
            swap(j, ch).wait_send()
    for j in range(1, 8):
        rs(j).wait_send()
    for j in range(1, ZS):
        zsum(j).wait_send()
    for dx, dz in others:
        spread_part(dx, dz).wait_send()
    for d in range(8):
        pl.when(me != d)(lambda: give(d).wait_send())
    for j in range(1, 8):
        remote(
            rows.at[pl.ds(0, 32)], out.at[:, :, mine], give_send.at[j], give_recv.at[j], dom, (me + j) % 8
        ).wait_recv()


def step_call(orb, seed, levels, sizes, centres):
    dma = pltpu.SemaphoreType.DMA
    vmem = pltpu.VMEM
    block = vmem((32, 8, 1024), F32)
    plane = vmem((8, 1024), F32)
    square = vmem((256, 256), F32)
    hbm = pl.BlockSpec(memory_space=pltpu.MemorySpace.HBM)
    return pl.pallas_call(
        step_kernel,
        out_shape=(
            jax.ShapeDtypeStruct((32, 8, 1024), F32),
            jax.ShapeDtypeStruct((256, 256), F32),
        ),
        in_specs=[hbm] * 5,
        out_specs=(VM, VM),
        scratch_shapes=[
            pltpu.SMEM((16,), F32), pltpu.SMEM((16,), jnp.int32), pltpu.SMEM((16,), F32),
            block, vmem((8, 1024), jnp.int32), block, block, vmem((8, 1024), jnp.int32),
            plane, plane, vmem((32, 128), F32), block,
            vmem((256, 8, 128), F32), vmem((256, 1024), F32), square, vmem((8, 32, 256), F32),
            vmem((8, 8, 128), F32), vmem((ZS, 8, 128), F32), vmem((XS, ZS, 8, 128), F32),
            square, square, vmem((BLOCK, 128), F32), vmem((256, 1024), F32), vmem((256, 8, 128), F32),
            dma((5,)), pltpu.SemaphoreType.REGULAR,
            dma((2, CHUNKS)), dma((2, CHUNKS)), dma((2,)), dma((2,)),
            dma((7, CHUNKS)), dma((7, CHUNKS)),
            dma((7,)), dma((7,)), dma((7,)), dma((7,)), dma((XS, ZS)), dma((XS, ZS)),
            dma((2, 7)), dma((2, 7)), dma((8,)), dma((8,)),
        ],
        compiler_params=pltpu.CompilerParams(
            collective_id=0, has_side_effects=True, vmem_limit_bytes=24 << 20
        ),
        name="filtered_step",
    )(*(pltpu.with_memory_space_constraint(a, pltpu.HBM) for a in (orb, seed, levels, sizes, centres)))


def finish_kernel(out, factor, out_h, factor_h, sem):
    copies = [
        pltpu.make_async_copy(out, out_h, sem.at[0]),
        pltpu.make_async_copy(factor, factor_h, sem.at[1]),
    ]
    for copy in copies:
        copy.start()
    for copy in copies:
        copy.wait()


def finish_call(out, factor):
    hbm = pl.BlockSpec(memory_space=pl.ANY)
    return pl.pallas_call(
        finish_kernel,
        out_shape=(
            jax.ShapeDtypeStruct((32, 8, 1024), F32),
            jax.ShapeDtypeStruct((256, 256), F32),
        ),
        in_specs=[VM, VM],
        out_specs=(hbm, hbm),
        scratch_shapes=[pltpu.SemaphoreType.DMA((2,))],
        compiler_params=pltpu.CompilerParams(vmem_limit_bytes=4 << 20),
        name="write_results",
    )(out, factor)


def shards(orbitals, seed_index, levels, group_sizes, centres):
    return finish_call(*step_call(orbitals, seed_index, levels, group_sizes, centres))


def solution(mesh):
    in_specs = (P("band", "domain", None), P("domain", None), P(), P(), P())
    out_specs = (P("band", "domain", None), P())
    return jax.shard_map(
        shards, mesh=mesh, in_specs=in_specs, out_specs=out_specs, check_vma=False
    )
```
